512 devices in a mesh: dp: 16 (over x, z_hi), code: 32 (over z_lo, y, core).
Axes of the slice: x: 4, y: 8, z: 8 (z_hi: 4, z_lo: 2; z = z_hi * 2 + z_lo), core: 2. Of those that a mesh axis runs over, the one named last changes fastest.
Arguments:
- tokens: bfloat16 [8192, 256], P('dp'), may hold values from -40 to 40
- codebook: bfloat16 [131072, 256], P('code'), may hold values from -6 to 6
- cotangent: bfloat16 [8192, 256], P('dp'), may hold values from -6 to 6
- index: int32 [8192], P('dp'), may hold values from 0 to 131071
Outputs:
- quantized: bfloat16 [8192, 256], P('dp')
- token_grad: bfloat16 [8192, 256], P('dp')
- codebook_grad: bfloat16 [131072, 256], P(('code', 'dp'))
- code_usage: float32 [131072], P(('code', 'dp'))
- entropy_loss: float32 [], replicated
The draws below stay inside these ranges and needn't reach their ends.
All inputs are finite; a program needn't handle non-finite values.
Results may differ from the reference program's by a relative error of at most 0.012.
Values may be sent and summed in bfloat16 or wider, within the bound.
A program may use at most 64 MiB of HBM per device.

```python
import jax
import jax.numpy as jnp
from jax import lax

CODE_WIDTH = 256
K = 131072
TOK_DEV = 512
TOKENS = 8192
N_DP = 16


def draw_codebook(key, part):
    own = jax.random.fold_in(key, 2)
    return jnp.clip(jax.random.normal(own, (K, CODE_WIDTH), jnp.float32), -6.0, 6.0).astype(jnp.bfloat16)


def draw_tokens(key, part):
    own = jax.random.fold_in(key, 1)
    return jnp.clip(jax.random.normal(own, (TOKENS, CODE_WIDTH), jnp.float32), -6.0, 6.0).astype(jnp.bfloat16)


def plant(values, stream_key, least, top_value):
    shape = values.shape
    index_at = [jax.random.randint(jax.random.fold_in(stream_key, axis), (), 0, shape[axis]) for axis in range(len(shape))]
    values = values.at[tuple(index_at)].set(least)
    longest = shape.index(max(shape))
    index_at[longest] = (index_at[longest] + 1) % shape[longest]
    return values.at[tuple(index_at)].set(top_value)


def block_levels(own_key, dims, pieces, smallest, high):
    loudness = 1.0
    for dim, blocks in pieces:
        heights = jax.random.uniform(jax.random.fold_in(jax.random.fold_in(own_key, 6), dim), (blocks,), jnp.float32, smallest / len(pieces), high / len(pieces))
        loudness = loudness * jnp.repeat(jnp.exp(heights), dims[dim] // blocks).reshape((-1,) + (1,) * (len(dims) - 1 - dim))
    return loudness


def scatter_about(stream_key, dims, scale, most, shards=(), kind=jnp.bfloat16):
    loudness = block_levels(stream_key, dims, shards, -0.22, 0.18) if shards else 1.0
    drawn = jax.random.normal(stream_key, dims, jnp.float32) * scale * loudness
    return jnp.minimum(jnp.maximum(drawn, -most), most).astype(kind)


def setup_inputs(seed: int = 0) -> dict:
    splits = jax.random.split(jax.random.key(seed), 5)
    tokens = draw_tokens(jax.random.fold_in(splits[4], 71), 0)
    codebook = draw_codebook(jax.random.fold_in(splits[4], 71), 0)
    cotangent = scatter_about(splits[2], (TOKENS, CODE_WIDTH), 1.0, 6.0, ((0, 16),))
    index = plant(jax.random.randint(splits[3], (TOKENS,), 0, K), jax.random.fold_in(splits[3], 1), 0, K - 1).astype(jnp.int32)
    return dict(tokens=tokens, codebook=codebook, cotangent=cotangent, index=index)


def reference(tokens, codebook, cotangent, index):
    scale_factor = float(CODE_WIDTH) ** -0.5
    block_length = min(K, 4096)
    block_count = K // block_length
    stacked = codebook.reshape(block_count, block_length, CODE_WIDTH)

    def block_totals(code_block):
        logits = jnp.dot(tokens, code_block.T, preferred_element_type=jnp.float32) * scale_factor
        sensed = jnp.dot(cotangent, code_block.T, preferred_element_type=jnp.float32)
        row_top = jnp.max(logits, axis=1)
        weights = jnp.exp(logits - row_top[:, None])
        return row_top, jnp.sum(weights, axis=1), jnp.sum(weights * sensed, axis=1), jnp.sum(weights * logits, axis=1)

    block_tops, block_sums, sensed_sums, logit_sums = lax.map(block_totals, stacked)
    row_peak = jnp.max(block_tops, axis=0)
    factor = jnp.exp(block_tops - row_peak[None, :])
    row_total = jnp.sum(block_sums * factor, axis=0)
    row_dot = jnp.sum(sensed_sums * factor, axis=0) / row_total
    mean_logit = jnp.sum(logit_sums * factor, axis=0) / row_total
    token_entropy = jnp.log(row_total) + row_peak - mean_logit

    token_block = (jnp.arange(TOKENS, dtype=jnp.int32) // TOK_DEV).astype(jnp.int32)
    token_matrix = tokens.astype(jnp.float32).reshape(N_DP, TOK_DEV, CODE_WIDTH)
    cotangent_wide = cotangent.astype(jnp.float32)

    def gradient_step(running, item):
        code_block, block_number = item
        logits = jnp.dot(tokens, code_block.T, preferred_element_type=jnp.float32) * scale_factor
        sensed = jnp.dot(cotangent, code_block.T, preferred_element_type=jnp.float32)
        probs = jnp.exp(logits - row_peak[:, None]) / row_total[:, None]
        logit_grad = (probs * (sensed - row_dot[:, None])).astype(jnp.bfloat16)
        running = running + jnp.dot(logit_grad, code_block, preferred_element_type=jnp.float32)
        local_ids = (index - block_number * block_length).astype(jnp.int32)
        inside = (local_ids >= 0) & (local_ids < block_length)
        segment_ids = jnp.where(inside, token_block * block_length + local_ids, N_DP * block_length).astype(jnp.int32)
        selected_codes = jax.ops.segment_sum(cotangent_wide, segment_ids, num_segments=N_DP * block_length + 1)[:-1]
        gradient_wide = logit_grad.astype(jnp.float32).reshape(N_DP, TOK_DEV, block_length)
        gradient_terms = scale_factor * jnp.einsum("ceu,cey->cuy", gradient_wide, token_matrix) + selected_codes.reshape(N_DP, block_length, CODE_WIDTH)
        gradient_terms = lax.optimization_barrier(gradient_terms.astype(jnp.bfloat16)).astype(jnp.float32)
        usage_terms = jnp.sum(probs.reshape(N_DP, TOK_DEV, block_length), axis=1)
        return running, (jnp.sum(gradient_terms, axis=0), jnp.sum(usage_terms, axis=0))

    running, outputs = lax.scan(gradient_step, jnp.zeros((TOKENS, CODE_WIDTH), jnp.float32),
                                (stacked, jnp.arange(block_count, dtype=jnp.int32)))
    token_grad = (running * scale_factor).astype(jnp.bfloat16)
    codebook_grad = outputs[0].reshape(K, CODE_WIDTH).astype(jnp.bfloat16)
    usage = outputs[1].reshape(K)
    code_usage = usage * (K / TOKENS)
    shares = usage / TOKENS
    entropy_loss = jnp.mean(token_entropy) + jnp.sum(jax.scipy.special.xlogy(shares, shares))
    quantized = jnp.take(codebook, index, axis=0)
    return quantized, token_grad, codebook_grad, code_usage, entropy_loss
```

```python
import functools

import jax
import jax.numpy as jnp
from jax import lax
from jax.experimental import pallas as pl
from jax.experimental.pallas import tpu as pltpu
from jax.sharding import PartitionSpec as P

MESH = pl.DeviceIdType.MESH
F32 = jnp.float32
BF16 = jnp.bfloat16
RING = 4
VMEM_BYTES = 60 * 1024 * 1024


def dot(a, b, dims):
    return lax.dot_general(a, b, (dims, ((), ())), preferred_element_type=F32)


def vmem():
    return pl.BlockSpec(memory_space=pltpu.VMEM)


def totals_kernel(scale, code_rows, tok_ref, cot_ref, idx_ref, cb_ref, st_ref, q_ref, run, qacc):
    step = pl.program_id(0)
    steps = pl.num_programs(0)
    block = cb_ref.shape[0]

    @pl.when(step == 0)
    def _():
        run[0:1, :] = jnp.full_like(run[0:1, :], -jnp.inf)
        run[1:4, :] = jnp.zeros_like(run[1:4, :])
        qacc[...] = jnp.zeros_like(qacc)

    codes = cb_ref[...]
    logits = dot(codes, tok_ref[...], ((1,), (1,)))
    sensed = dot(codes, cot_ref[...], ((1,), (1,)))
    old = run[0:1, :]
    top = jnp.maximum(old, jnp.max(logits, axis=0, keepdims=True))
    weights = jnp.exp((logits - top) * scale)
    factor = jnp.exp((old - top) * scale)
    run[0:1, :] = top
    run[1:2, :] = run[1:2, :] * factor + jnp.sum(weights, axis=0, keepdims=True)
    run[2:3, :] = run[2:3, :] * factor + jnp.sum(weights * sensed, axis=0, keepdims=True)
    run[3:4, :] = run[3:4, :] * factor + jnp.sum(weights * logits, axis=0, keepdims=True)
    first = lax.axis_index("code") * code_rows + step * block
    rows = lax.broadcasted_iota(jnp.int32, logits.shape, 0)
    hot = jnp.where(rows == idx_ref[...] - first, 1.0, 0.0).astype(BF16)
    qacc[...] += dot(codes, hot, ((0,), (0,)))

    @pl.when(step == steps - 1)
    def _():
        st_ref[...] = run[...]
        q_ref[...] = qacc[...].T.astype(BF16)


def totals(tokens, cotangent, index, codebook, scale, block):
    rows, width = tokens.shape
    code_rows = codebook.shape[0]
    whole = lambda i: (0, 0)
    return pl.pallas_call(
        functools.partial(totals_kernel, scale, code_rows),
        grid=(code_rows // block,),
        out_shape=(
            jax.ShapeDtypeStruct((4, rows), F32),
            jax.ShapeDtypeStruct((rows, width), BF16),
        ),
        in_specs=[
            pl.BlockSpec((rows, width), whole),
            pl.BlockSpec((rows, width), whole),
            pl.BlockSpec((1, rows), whole),
            pl.BlockSpec((block, width), lambda i: (i, 0)),
        ],
        out_specs=(pl.BlockSpec((4, rows), whole), pl.BlockSpec((rows, width), whole)),
        scratch_shapes=[pltpu.VMEM((4, rows), F32), pltpu.VMEM((width, rows), F32)],
        compiler_params=pltpu.CompilerParams(vmem_limit_bytes=VMEM_BYTES),
        name="totals",
    )(tokens, cotangent, index, codebook)


def stats_kernel(scale, chips, st_ref, out_ref, pair_buf, mine, chip_buf, psend, precv, send, recv):
    dp = lax.axis_index("dp")
    code = lax.axis_index("code")
    core, chip = code % 2, code // 2
    partner = (dp, chip * 2 + 1 - core)
    peers = [(dp, ((chip + j) % chips) * 2 + core) for j in range(1, chips)]
    barrier = pltpu.get_barrier_semaphore()
    for peer in [partner] + peers:
        pl.semaphore_signal(barrier, inc=1, device_id=peer, device_id_type=MESH)
    pl.semaphore_wait(barrier, chips)

    swap = pltpu.make_async_remote_copy(
        src_ref=st_ref, dst_ref=pair_buf, send_sem=psend, recv_sem=precv,
        device_id=partner, device_id_type=MESH,
    )
    swap.start()
    swap.wait()
    one, two = st_ref[...], pair_buf[...]
    top = jnp.maximum(one[0:1], two[0:1])
    sums = one[1:4] * jnp.exp((one[0:1] - top) * scale) + two[1:4] * jnp.exp((two[0:1] - top) * scale)
    mine[0:1, :] = top
    mine[1:4, :] = sums
    copies = []
    for j, peer in enumerate(peers):
        copy = pltpu.make_async_remote_copy(
            src_ref=mine, dst_ref=chip_buf.at[chip], send_sem=send.at[j], recv_sem=recv.at[j],
            device_id=peer, device_id_type=MESH,
        )
        copy.start()
        copies.append(copy)
    chip_buf[pl.ds(chip, 1), :, :] = mine[...][None]
    for copy in copies:
        copy.wait()
    tops = [chip_buf[j, 0:1, :] for j in range(chips)]
    peak = functools.reduce(jnp.maximum, tops)
    total = sum(chip_buf[j, 1:4, :] * jnp.exp((tops[j] - peak) * scale) for j in range(chips))
    weight = total[0:1]
    inverse = 1.0 / weight
    out_ref[0:1, :] = peak
    out_ref[1:2, :] = inverse
    out_ref[2:3, :] = total[1:2] / weight
    out_ref[3:4, :] = jnp.log(weight) + (peak - total[2:3] / weight) * scale


def row_stats(local, scale, chips):
    shape = local.shape
    return pl.pallas_call(
        functools.partial(stats_kernel, scale, chips),
        out_shape=jax.ShapeDtypeStruct(shape, F32),
        in_specs=[vmem()],
        out_specs=vmem(),
        scratch_shapes=[
            pltpu.VMEM(shape, F32),
            pltpu.VMEM(shape, F32),
            pltpu.VMEM((chips,) + shape, F32),
            pltpu.SemaphoreType.DMA,
            pltpu.SemaphoreType.DMA,
            pltpu.SemaphoreType.DMA((chips - 1,)),
            pltpu.SemaphoreType.DMA((chips - 1,)),
        ],
        compiler_params=pltpu.CompilerParams(collective_id=0, has_side_effects=True),
        name="row_stats",
    )(local)


def grads_kernel(scale, code_rows, tok_ref, cot_ref, idx_ref, st_ref, cb_ref, cg_ref, us_ref, tg_ref, acc):
    step = pl.program_id(0)
    steps = pl.num_programs(0)
    block = cb_ref.shape[0]

    @pl.when(step == 0)
    def _():
        acc[...] = jnp.zeros_like(acc)

    codes = cb_ref[...]
    tok = tok_ref[...]
    cot = cot_ref[...]
    logits = dot(codes, tok, ((1,), (1,)))
    sensed = dot(codes, cot, ((1,), (1,)))
    probs = jnp.exp((logits - st_ref[0:1, :]) * scale) * st_ref[1:2, :]
    grad = (probs * (sensed - st_ref[2:3, :])).astype(BF16)
    acc[...] += dot(codes, grad, ((0,), (0,)))
    first = lax.axis_index("code") * code_rows + step * block
    rows = lax.broadcasted_iota(jnp.int32, logits.shape, 0)
    hot = jnp.where(rows == idx_ref[...] - first, 1.0, 0.0).astype(BF16)
    cg_ref[...] = (dot(grad, tok, ((1,), (0,))) * scale + dot(hot, cot, ((1,), (0,)))).astype(BF16)
    lanes = min(128, probs.shape[1])
    part = sum(probs[:, i : i + lanes] for i in range(0, probs.shape[1], lanes))
    usage = jnp.sum(part.T, axis=0, keepdims=True)
    span = us_ref.shape[2]
    for i in range(us_ref.shape[0]):
        us_ref[i, :, :] = usage[:, i * span : (i + 1) * span]

    @pl.when(step == steps - 1)
    def _():
        tg_ref[...] = (acc[...] * scale).T.astype(BF16)


def grads(tokens, cotangent, index, stats, codebook, scale, block, data_devices):
    rows, width = tokens.shape
    code_rows = codebook.shape[0]
    span = code_rows // data_devices
    whole = lambda i: (0, 0)
    return pl.pallas_call(
        functools.partial(grads_kernel, scale, code_rows),
        grid=(code_rows // block,),
        out_shape=(
            jax.ShapeDtypeStruct((code_rows, width), BF16),
            jax.ShapeDtypeStruct((data_devices, 1, span), F32),
            jax.ShapeDtypeStruct((rows, width), BF16),
        ),
        in_specs=[
            pl.BlockSpec((rows, width), whole),
            pl.BlockSpec((rows, width), whole),
            pl.BlockSpec((1, rows), whole),
            pl.BlockSpec((4, rows), whole),
            pl.BlockSpec((block, width), lambda i: (i, 0)),
        ],
        out_specs=(
            pl.BlockSpec((block, width), lambda i: (i, 0)),
            pl.BlockSpec((block // span, 1, span), lambda i: (i, 0, 0)),
            pl.BlockSpec((rows, width), whole),
        ),
        scratch_shapes=[pltpu.VMEM((width, rows), F32)],
        compiler_params=pltpu.CompilerParams(vmem_limit_bytes=VMEM_BYTES),
        name="grads",
    )(tokens, cotangent, index, stats, codebook)


def sums_kernel(
    chips, tokens_total, codes_total,
    q_ref, tg_ref, cg_ref, us_ref, st_ref,
    qo_ref, tgo_ref, cgo_ref, uso_ref, loss_ref,
    t_in, t_half, t_piece, t_sum, t_full,
    x_hop, x_out, x_got, z_part, z_hop, z_out, z_got,
    u_buf, l_own, l_dp, l_core, l_pair, l_chip,
    t_send, t_recv, p_send, p_recv, g_send, g_recv, f_send, f_recv,
    x_send, x_recv, z_send, z_recv,
    u_send, u_recv, ld_send, ld_recv, lc_send, lc_recv, lg_send, lg_recv,
):
    dp = lax.axis_index("dp")
    code = lax.axis_index("code")
    core, chip = code % 2, code // 2
    xi, zi = dp // RING, dp % RING
    data = RING * RING
    rows = q_ref.shape[0]
    half = rows // 2
    piece = half // chips
    span = cg_ref.shape[0] // data
    hs = span // 2

    partner = (dp, chip * 2 + 1 - core)
    peers = [(dp, ((chip + j) % chips) * 2 + core) for j in range(1, chips)]
    mates = [((dp + j) % data, code) for j in range(1, data)]
    xn = {d: (((xi + d) % RING) * RING + zi, code) for d in (1, 3)}
    zn = {d: (xi * RING + (zi + d) % RING, code) for d in (1, 3)}

    barrier = pltpu.get_barrier_semaphore()
    for peer in [partner] + peers + mates:
        pl.semaphore_signal(barrier, inc=1, device_id=peer, device_id_type=MESH)
    pl.semaphore_wait(barrier, chips + data - 1)

    def send(src, dst, ssem, rsem, peer):
        copy = pltpu.make_async_remote_copy(
            src_ref=src, dst_ref=dst, send_sem=ssem, recv_sem=rsem, device_id=peer, device_id_type=MESH
        )
        copy.start()
        return copy

    u_copies = [
        send(us_ref.at[(dp + j) % data], u_buf.at[dp], u_send.at[j - 1], u_recv.at[j - 1], mates[j - 1])
        for j in range(1, data)
    ]
    theirs = pl.ds(pl.multiple_of((1 - core) * half, half), half)
    ours = pl.ds(pl.multiple_of(core * half, half), half)
    t_copies = [
        send(ref.at[theirs], t_in.at[i], t_send.at[i], t_recv.at[i], partner)
        for i, ref in enumerate((tg_ref, q_ref))
    ]

    order = [(zi + d) % RING for d in (2, 1, 3, 0)]
    x_copies = {}
    z_copies = {}

    def part(xd, k, side):
        start = (((xi + xd) % RING) * RING + order[k]) * span + side * hs
        return pl.ds(pl.multiple_of(start, hs), hs)

    def x_first(k):
        x_copies[k, 0] = send(cg_ref.at[part(2, k, 0)], x_hop.at[k, 0], x_send.at[k, 0], x_recv.at[k, 0], xn[1])
        x_copies[k, 1] = send(cg_ref.at[part(2, k, 1)], x_hop.at[k, 1], x_send.at[k, 1], x_recv.at[k, 1], xn[3])

    def x_direct(k):
        x_copies[k, 2] = send(cg_ref.at[part(1, k, 1)], x_got.at[k, 1], x_send.at[k, 2], x_recv.at[k, 2], xn[1])
        x_copies[k, 3] = send(cg_ref.at[part(3, k, 0)], x_got.at[k, 0], x_send.at[k, 3], x_recv.at[k, 3], xn[3])

    def x_second(k):
        x_copies[k, 0].wait_recv()
        x_out[k, 0] = (x_hop[k, 0].astype(F32) + cg_ref[part(1, k, 0), :].astype(F32)).astype(BF16)
        x_copies[k, 4] = send(x_out.at[k, 0], x_got.at[k, 3], x_send.at[k, 4], x_recv.at[k, 4], xn[1])
        x_copies[k, 1].wait_recv()
        x_out[k, 1] = (x_hop[k, 1].astype(F32) + cg_ref[part(3, k, 1), :].astype(F32)).astype(BF16)
        x_copies[k, 5] = send(x_out.at[k, 1], x_got.at[k, 2], x_send.at[k, 5], x_recv.at[k, 5], xn[3])

    def x_third(k):
        for i in (2, 3, 4, 5):
            x_copies[k, i].wait_recv()
        low = cg_ref[part(0, k, 0), :].astype(F32) + x_got[k, 0].astype(F32) + x_got[k, 3].astype(F32)
        high = cg_ref[part(0, k, 1), :].astype(F32) + x_got[k, 1].astype(F32) + x_got[k, 2].astype(F32)
        return low, high

    def z_store(k):
        low, high = x_third(k)
        z_part[k, 0] = low.astype(BF16)
        z_part[k, 1] = high.astype(BF16)

    def z_first():
        z_store(0)
        z_copies[0] = send(z_part.at[0, 0], z_hop.at[0], z_send.at[0], z_recv.at[0], zn[1])
        z_copies[1] = send(z_part.at[0, 1], z_hop.at[1], z_send.at[1], z_recv.at[1], zn[3])

    def z_second_up():
        z_store(1)
        z_copies[2] = send(z_part.at[1, 1], z_got.at[1], z_send.at[2], z_recv.at[2], zn[1])
        z_copies[0].wait_recv()
        z_out[0] = (z_hop[0].astype(F32) + z_part[1, 0].astype(F32)).astype(BF16)
        z_copies[4] = send(z_out.at[0], z_got.at[3], z_send.at[4], z_recv.at[4], zn[1])

    def z_second_down():
        z_store(2)
        z_copies[3] = send(z_part.at[2, 0], z_got.at[0], z_send.at[3], z_recv.at[3], zn[3])
        z_copies[1].wait_recv()
        z_out[1] = (z_hop[1].astype(F32) + z_part[2, 1].astype(F32)).astype(BF16)
        z_copies[5] = send(z_out.at[1], z_got.at[2], z_send.at[5], z_recv.at[5], zn[3])

    def z_third():
        low, high = x_third(3)
        for i in (2, 3, 4, 5):
            z_copies[i].wait_recv()
        cgo_ref[0:hs, :] = (low + z_got[0].astype(F32) + z_got[3].astype(F32)).astype(BF16)
        cgo_ref[hs:, :] = (high + z_got[1].astype(F32) + z_got[2].astype(F32)).astype(BF16)

    x_first(0)
    x_direct(0)
    x_first(1)

    for i, ref in enumerate((tg_ref, q_ref)):
        t_copies[i].wait_recv()
        t_half[i] = (t_in[i].astype(F32) + ref[ours, :].astype(F32)).astype(BF16)

    def rows_of(j):
        return pl.ds(pl.multiple_of(((chip + j) % chips) * piece, piece), piece)

    p_copies = [
        send(t_half.at[:, rows_of(j)], t_piece.at[j], p_send.at[j - 1], p_recv.at[j - 1], peers[j - 1])
        for j in range(1, chips)
    ]

    x_second(0)
    x_direct(1)
    x_first(2)

    u_buf[pl.ds(dp, 1), :, :] = us_ref[pl.ds(dp, 1), :, :]
    for copy in u_copies:
        copy.wait_recv()
    usage = sum(u_buf[j] for j in range(data))
    uso_ref[...] = usage * (codes_total / tokens_total)
    shares = usage / tokens_total
    terms = jnp.where(shares > 0, shares * jnp.log(jnp.where(shares > 0, shares, 1.0)), 0.0)
    local = jnp.sum(st_ref[3:4, :]) / (tokens_total * chips * 2) + jnp.sum(terms)
    l_own[...] = jnp.full(l_own.shape, local, F32)
    l_dp[pl.ds(dp, 1), :, :] = l_own[...][None]
    ld_copies = [
        send(l_own, l_dp.at[dp], ld_send.at[j - 1], ld_recv.at[j - 1], mates[j - 1]) for j in range(1, data)
    ]

    x_second(1)
    x_direct(2)
    x_first(3)

    for copy in p_copies:
        copy.wait_recv()
    mine = rows_of(0)
    total = t_half[:, mine, :].astype(F32)
    for j in range(1, chips):
        total = total + t_piece[j].astype(F32)
    t_sum[...] = total.astype(BF16)
    base = core * half
    spot = pl.ds(pl.multiple_of(base + chip * piece, piece), piece)
    g_copies = [
        send(t_sum, t_full.at[:, spot], g_send.at[j - 1], g_recv.at[j - 1], peers[j - 1]) for j in range(1, chips)
    ]
    t_full[:, spot, :] = t_sum[...]

    z_first()
    x_second(2)
    x_direct(3)

    for copy in ld_copies:
        copy.wait_recv()
    l_core[...] = sum(l_dp[j] for j in range(data))
    lc_copy = send(l_core, l_pair, lc_send, lc_recv, partner)

    z_second_up()
    x_second(3)

    for copy in g_copies:
        copy.wait_recv()
    f_copy = send(t_full.at[:, ours], t_full.at[:, ours], f_send, f_recv, partner)

    lc_copy.wait_recv()
    l_chip[pl.ds(chip, 1), :, :] = (l_core[...] + l_pair[...])[None]
    lg_copies = [
        send(l_chip.at[chip], l_chip.at[chip], lg_send.at[j - 1], lg_recv.at[j - 1], peers[j - 1])
        for j in range(1, chips)
    ]

    z_second_down()
    z_third()

    f_copy.wait_recv()
    tgo_ref[...] = t_full[0]
    qo_ref[...] = t_full[1]
    for copy in lg_copies:
        copy.wait_recv()
    loss_ref[...] = sum(l_chip[j] for j in range(chips))

    pending = u_copies + t_copies + p_copies + ld_copies + g_copies + lg_copies + [lc_copy, f_copy]
    for copy in pending + list(x_copies.values()) + list(z_copies.values()):
        copy.wait_send()


def final_sums(q_part, tg_part, cg_part, usage_part, stats, chips, tokens_total, codes_total):
    rows, width = q_part.shape
    data = RING * RING
    span = cg_part.shape[0] // data
    hs = span // 2
    half = rows // 2
    piece = half // chips
    dma = pltpu.SemaphoreType.DMA
    return pl.pallas_call(
        functools.partial(sums_kernel, chips, tokens_total, codes_total),
        out_shape=(
            jax.ShapeDtypeStruct((rows, width), BF16),
            jax.ShapeDtypeStruct((rows, width), BF16),
            jax.ShapeDtypeStruct((span, width), BF16),
            jax.ShapeDtypeStruct((1, span), F32),
            jax.ShapeDtypeStruct((1, 128), F32),
        ),
        in_specs=[vmem()] * 5,
        out_specs=(vmem(),) * 5,
        scratch_shapes=[
            pltpu.VMEM((2, half, width), BF16),
            pltpu.VMEM((2, half, width), BF16),
            pltpu.VMEM((chips, 2, piece, width), BF16),
            pltpu.VMEM((2, piece, width), BF16),
            pltpu.VMEM((2, rows, width), BF16),
            pltpu.VMEM((RING, 2, hs, width), BF16),
            pltpu.VMEM((RING, 2, hs, width), BF16),
            pltpu.VMEM((RING, 4, hs, width), BF16),
            pltpu.VMEM((RING - 1, 2, hs, width), BF16),
            pltpu.VMEM((2, hs, width), BF16),
            pltpu.VMEM((2, hs, width), BF16),
            pltpu.VMEM((4, hs, width), BF16),
            pltpu.VMEM((data, 1, span), F32),
            pltpu.VMEM((1, 128), F32),
            pltpu.VMEM((data, 1, 128), F32),
            pltpu.VMEM((1, 128), F32),
            pltpu.VMEM((1, 128), F32),
            pltpu.VMEM((chips, 1, 128), F32),
            dma((2,)), dma((2,)),
            dma((chips - 1,)), dma((chips - 1,)),
            dma((chips - 1,)), dma((chips - 1,)),
            dma, dma,
            dma((RING, 6)), dma((RING, 6)),
            dma((6,)), dma((6,)),
            dma((data - 1,)), dma((data - 1,)),
            dma((data - 1,)), dma((data - 1,)),
            dma, dma,
            dma((chips - 1,)), dma((chips - 1,)),
        ],
        compiler_params=pltpu.CompilerParams(
            collective_id=1, has_side_effects=True, vmem_limit_bytes=VMEM_BYTES
        ),
        name="final_sums",
    )(q_part, tg_part, cg_part, usage_part, stats)


def body(block, tokens, codebook, cotangent, index):
    token_rows, features = tokens.shape
    code_rows = codebook.shape[0]
    scale = float(features) ** (-0.5)
    code_devices = lax.axis_size("code")
    data_devices = lax.axis_size("dp")
    chips = code_devices // 2
    index = index.reshape(1, token_rows)
    local, q_part = totals(tokens, cotangent, index, codebook, scale, block)
    stats = row_stats(local, scale, chips)
    cg_part, usage_part, tg_part = grads(
        tokens, cotangent, index, stats, codebook, scale, block, data_devices
    )
    quantized, token_grad, code_sum, code_usage, loss = final_sums(
        q_part, tg_part, cg_part, usage_part, stats, chips,
        token_rows * data_devices, code_rows * code_devices,
    )
    return (quantized, token_grad, code_sum, code_usage.reshape(-1), loss[0, 0])


def solution(mesh, block=512):
    placed = (P("dp", None), P("code", None), P("dp", None), P("dp"))
    return jax.shard_map(
        functools.partial(body, block),
        mesh=mesh,
        in_specs=placed,
        out_specs=(P("dp", None), P("dp", None), P(("code", "dp"), None), P(("code", "dp")), P()),
        check_vma=False,
    )
```

```python
import functools

import jax
import jax.numpy as jnp
from jax import lax
from jax.experimental import pallas as pl
from jax.experimental.pallas import tpu as pltpu
from jax.sharding import PartitionSpec as P

MESH = pl.DeviceIdType.MESH
F32 = jnp.float32
BF16 = jnp.bfloat16
RING = 4
VMEM_BYTES = 60 * 1024 * 1024


def dot(a, b, dims):
    return lax.dot_general(a, b, (dims, ((), ())), preferred_element_type=F32)


def vmem():
    return pl.BlockSpec(memory_space=pltpu.VMEM)


def fused_kernel(
    scale, code_rows, block, chips, tokens_total, codes_total,
    tok_ref, cot_ref, idx_ref, cb_hbm,
    qo_ref, tgo_ref, cgo_ref, uso_ref, loss_ref,
    cb_ref, w_buf, s_buf, ch_buf, cg_ref, us_ref, tops, run, acc, qt_ref,
    pair_buf, mine_buf, chip_buf, stats,
    t_in, t_half, t_piece, t_sum, t_full,
    x_hop, x_out, x_got, z_part, z_hop, z_out, z_got,
    u_buf, l_own, l_dp, l_core, l_pair, l_chip,
    cb_sem, s_send, s_recv, st_send, st_recv,
    t_send, t_recv, p_send, p_recv, g_send, g_recv, f_send, f_recv,
    x_send, x_recv, z_send, z_recv,
    u_send, u_recv, ld_send, ld_recv, lc_send, lc_recv, lg_send, lg_recv,
):
    dp = lax.axis_index("dp")
    code = lax.axis_index("code")
    core, chip = code % 2, code // 2
    xi, zi = dp // RING, dp % RING
    data = RING * RING
    blocks = code_rows // block
    rows = tok_ref.shape[0]
    half = rows // 2
    piece = half // chips
    span = code_rows // data
    hs = span // 2
    first_code = code * code_rows

    def load(i):
        part = pl.ds(pl.multiple_of(i * block, block), block)
        return pltpu.make_async_copy(cb_hbm.at[part], cb_ref.at[part], cb_sem.at[i])

    for i in range(blocks):
        load(i).start()

    partner = (dp, chip * 2 + 1 - core)
    peers = [(dp, ((chip + j) % chips) * 2 + core) for j in range(1, chips)]
    mates = [((dp + j) % data, code) for j in range(1, data)]
    xn = {d: (((xi + d) % RING) * RING + zi, code) for d in (1, 3)}
    zn = {d: (xi * RING + (zi + d) % RING, code) for d in (1, 3)}

    barrier = pltpu.get_barrier_semaphore()
    for peer in [partner] + peers + mates:
        pl.semaphore_signal(barrier, inc=1, device_id=peer, device_id_type=MESH)

    pending = []

    def send(src, dst, ssem, rsem, peer):
        copy = pltpu.make_async_remote_copy(
            src_ref=src, dst_ref=dst, send_sem=ssem, recv_sem=rsem, device_id=peer, device_id_type=MESH
        )
        copy.start()
        pending.append(copy)
        return copy

    run[0:1, :] = jnp.full((1, rows), -jnp.inf, F32)
    run[1:4, :] = jnp.zeros((3, rows), F32)

    def totals(i, carry):
        load(i).wait()
        part = pl.ds(pl.multiple_of(i * block, block), block)
        codes = cb_ref[part, :]
        logits = dot(codes, tok_ref[...], ((1,), (1,)))
        sensed = dot(codes, cot_ref[...], ((1,), (1,)))
        old = run[0:1, :]
        top = jnp.maximum(old, jnp.max(logits, axis=0, keepdims=True))
        weights = jnp.exp((logits - top) * scale)
        factor = jnp.exp((old - top) * scale)
        w_buf[part, :] = weights
        s_buf[part, :] = sensed
        tops[i] = top
        run[0:1, :] = top
        run[1:2, :] = run[1:2, :] * factor + jnp.sum(weights, axis=0, keepdims=True)
        run[2:3, :] = run[2:3, :] * factor + jnp.sum(weights * sensed, axis=0, keepdims=True)
        run[3:4, :] = run[3:4, :] * factor + jnp.sum(weights * logits, axis=0, keepdims=True)
        return carry

    lax.fori_loop(0, blocks, totals, 0)

    pl.semaphore_wait(barrier, chips + data - 1)
    swap = send(run, pair_buf, s_send, s_recv, partner)

    acc[...] = jnp.zeros_like(acc)

    def picks(i, carry):
        part = pl.ds(pl.multiple_of(i * block, block), block)
        ids = lax.broadcasted_iota(jnp.int32, (block, rows), 0)
        hot = jnp.where(ids == idx_ref[...] - (first_code + i * block), 1.0, 0.0).astype(BF16)
        acc[...] += dot(cb_ref[part, :], hot, ((0,), (0,)))
        ch_buf[part, :] = dot(hot, cot_ref[...], ((1,), (0,)))
        return carry

    lax.fori_loop(0, blocks // 4, picks, 0)

    swap.wait_recv()
    one, two = run[...], pair_buf[...]
    top = jnp.maximum(one[0:1], two[0:1])
    mine_buf[0:1, :] = top
    mine_buf[1:4, :] = one[1:4] * jnp.exp((one[0:1] - top) * scale) + two[1:4] * jnp.exp((two[0:1] - top) * scale)
    st_copies = [
        send(mine_buf, chip_buf.at[chip], st_send.at[j - 1], st_recv.at[j - 1], peers[j - 1])
        for j in range(1, chips)
    ]
    chip_buf[pl.ds(chip, 1), :, :] = mine_buf[...][None]

    lax.fori_loop(blocks // 4, blocks, picks, 0)

    theirs = pl.ds(pl.multiple_of((1 - core) * half, half), half)
    ours = pl.ds(pl.multiple_of(core * half, half), half)

    def rows_of(j):
        return pl.ds(pl.multiple_of(((chip + j) % chips) * piece, piece), piece)

    def t_core(a):
        return send(qt_ref.at[a, theirs], t_in.at[a], t_send.at[a], t_recv.at[a], partner)

    def t_scatter(a, copy):
        copy.wait_recv()
        t_half[a] = (t_in[a].astype(F32) + qt_ref[a, ours, :].astype(F32)).astype(BF16)
        return [
            send(t_half.at[a, rows_of(j)], t_piece.at[a, j], p_send.at[a, j - 1], p_recv.at[a, j - 1], peers[j - 1])
            for j in range(1, chips)
        ]

    def t_gather(a, copies):
        for copy in copies:
            copy.wait_recv()
        total = t_half[a, rows_of(0), :].astype(F32)
        for j in range(1, chips):
            total = total + t_piece[a, j].astype(F32)
        t_sum[a] = total.astype(BF16)
        spot = pl.ds(pl.multiple_of(core * half + chip * piece, piece), piece)
        sent = [
            send(t_sum.at[a], t_full.at[a, spot], g_send.at[a, j - 1], g_recv.at[a, j - 1], peers[j - 1])
            for j in range(1, chips)
        ]
        t_full[a, spot, :] = t_sum[a]
        return sent

    def t_share(a, copies):
        for copy in copies:
            copy.wait_recv()
        return send(t_full.at[a, ours], t_full.at[a, ours], f_send.at[a], f_recv.at[a], partner)

    qt_ref[1] = acc[...].T.astype(BF16)
    q_copy = t_core(1)
    acc[...] = jnp.zeros_like(acc)

    for copy in st_copies:
        copy.wait_recv()
    peaks = [chip_buf[j, 0:1, :] for j in range(chips)]
    peak = functools.reduce(jnp.maximum, peaks)
    total = sum(chip_buf[j, 1:4, :] * jnp.exp((peaks[j] - peak) * scale) for j in range(chips))
    weight = total[0:1]
    stats[0:1, :] = peak
    stats[1:2, :] = 1.0 / weight
    stats[2:3, :] = total[1:2] / weight
    stats[3:4, :] = jnp.log(weight) + (peak - total[2:3] / weight) * scale

    order = [(zi + d) % RING for d in (2, 1, 3, 0)]
    lanes = min(128, rows)

    def units(k, low, high):
        def unit(i, carry):
            owner = ((xi + 6 - i) % RING) * RING + order[k]
            start = owner * span
            part = pl.ds(pl.multiple_of(start, span), span)
            level = jnp.exp((tops[start // block] - stats[0:1, :]) * scale) * stats[1:2, :]
            probs = w_buf[part, :] * level
            grad = (probs * (s_buf[part, :] - stats[2:3, :])).astype(BF16)
            acc[...] += dot(cb_ref[part, :], grad, ((0,), (0,)))
            cg_ref[part, :] = (dot(grad, tok_ref[...], ((1,), (0,))) * scale + ch_buf[part, :]).astype(BF16)
            folded = sum(probs[:, c : c + lanes] for c in range(0, rows, lanes))
            us_ref[owner] = jnp.sum(folded.T, axis=0, keepdims=True)
            return carry

        lax.fori_loop(low, high, unit, 0)

    x_copies = {}
    z_copies = {}

    def part(xd, k, side):
        start = (((xi + xd) % RING) * RING + order[k]) * span + side * hs
        return pl.ds(pl.multiple_of(start, hs), hs)

    def x_first(k):
        x_copies[k, 0] = send(cg_ref.at[part(2, k, 0)], x_hop.at[k, 0], x_send.at[k, 0], x_recv.at[k, 0], xn[1])
        x_copies[k, 1] = send(cg_ref.at[part(2, k, 1)], x_hop.at[k, 1], x_send.at[k, 1], x_recv.at[k, 1], xn[3])

    def x_direct(k):
        x_copies[k, 2] = send(cg_ref.at[part(1, k, 1)], x_got.at[k, 1], x_send.at[k, 2], x_recv.at[k, 2], xn[1])
        x_copies[k, 3] = send(cg_ref.at[part(3, k, 0)], x_got.at[k, 0], x_send.at[k, 3], x_recv.at[k, 3], xn[3])

    def x_second(k):
        x_copies[k, 0].wait_recv()
        x_out[k, 0] = (x_hop[k, 0].astype(F32) + cg_ref[part(1, k, 0), :].astype(F32)).astype(BF16)
        x_copies[k, 4] = send(x_out.at[k, 0], x_got.at[k, 3], x_send.at[k, 4], x_recv.at[k, 4], xn[1])
        x_copies[k, 1].wait_recv()
        x_out[k, 1] = (x_hop[k, 1].astype(F32) + cg_ref[part(3, k, 1), :].astype(F32)).astype(BF16)
        x_copies[k, 5] = send(x_out.at[k, 1], x_got.at[k, 2], x_send.at[k, 5], x_recv.at[k, 5], xn[3])

    def x_third(k):
        for i in (2, 3, 4, 5):
            x_copies[k, i].wait_recv()
        low = cg_ref[part(0, k, 0), :].astype(F32) + x_got[k, 0].astype(F32) + x_got[k, 3].astype(F32)
        high = cg_ref[part(0, k, 1), :].astype(F32) + x_got[k, 1].astype(F32) + x_got[k, 2].astype(F32)
        return low, high

    def z_store(k):
        low, high = x_third(k)
        z_part[k, 0] = low.astype(BF16)
        z_part[k, 1] = high.astype(BF16)

    def z_first():
        z_store(0)
        z_copies[0] = send(z_part.at[0, 0], z_hop.at[0], z_send.at[0], z_recv.at[0], zn[1])
        z_copies[1] = send(z_part.at[0, 1], z_hop.at[1], z_send.at[1], z_recv.at[1], zn[3])

    def z_second_up():
        z_store(1)
        z_copies[2] = send(z_part.at[1, 1], z_got.at[1], z_send.at[2], z_recv.at[2], zn[1])
        z_copies[0].wait_recv()
        z_out[0] = (z_hop[0].astype(F32) + z_part[1, 0].astype(F32)).astype(BF16)
        z_copies[4] = send(z_out.at[0], z_got.at[3], z_send.at[4], z_recv.at[4], zn[1])

    def z_second_down():
        z_store(2)
        z_copies[3] = send(z_part.at[2, 0], z_got.at[0], z_send.at[3], z_recv.at[3], zn[3])
        z_copies[1].wait_recv()
        z_out[1] = (z_hop[1].astype(F32) + z_part[2, 1].astype(F32)).astype(BF16)
        z_copies[5] = send(z_out.at[1], z_got.at[2], z_send.at[5], z_recv.at[5], zn[3])

    def z_third():
        low, high = x_third(3)
        for i in (2, 3, 4, 5):
            z_copies[i].wait_recv()
        cgo_ref[0:hs, :] = (low + z_got[0].astype(F32) + z_got[3].astype(F32)).astype(BF16)
        cgo_ref[hs:, :] = (high + z_got[1].astype(F32) + z_got[2].astype(F32)).astype(BF16)

    units(0, 0, 1)
    x_first(0)
    q_copies = t_scatter(1, q_copy)
    units(0, 1, 4)
    x_direct(0)
    units(1, 0, 4)
    x_first(1)
    x_second(0)
    x_direct(1)
    q_copies = t_gather(1, q_copies)
    units(2, 0, 4)
    x_first(2)
    x_second(1)
    x_direct(2)
    q_copy = t_share(1, q_copies)
    units(3, 0, 4)

    qt_ref[0] = (acc[...] * scale).T.astype(BF16)
    g_copy = t_core(0)
    u_copies = [
        send(us_ref.at[(dp + j) % data], u_buf.at[dp], u_send.at[j - 1], u_recv.at[j - 1], mates[j - 1])
        for j in range(1, data)
    ]
    u_buf[pl.ds(dp, 1), :, :] = us_ref[pl.ds(dp, 1), :, :]
    x_first(3)
    x_second(2)
    x_direct(3)
    g_copies = t_scatter(0, g_copy)
    z_first()

    for copy in u_copies:
        copy.wait_recv()
    usage = sum(u_buf[j] for j in range(data))
    uso_ref[...] = usage * (codes_total / tokens_total)
    shares = usage / tokens_total
    terms = jnp.where(shares > 0, shares * jnp.log(jnp.where(shares > 0, shares, 1.0)), 0.0)
    local = jnp.sum(stats[3:4, :]) / (tokens_total * chips * 2) + jnp.sum(terms)
    l_own[...] = jnp.full(l_own.shape, local, F32)
    l_dp[pl.ds(dp, 1), :, :] = l_own[...][None]
    ld_copies = [
        send(l_own, l_dp.at[dp], ld_send.at[j - 1], ld_recv.at[j - 1], mates[j - 1]) for j in range(1, data)
    ]

    x_second(3)
    z_second_up()
    g_copies = t_gather(0, g_copies)

    for copy in ld_copies:
        copy.wait_recv()
    l_core[...] = sum(l_dp[j] for j in range(data))
    lc_copy = send(l_core, l_pair, lc_send, lc_recv, partner)

    z_second_down()
    g_copy = t_share(0, g_copies)

    lc_copy.wait_recv()
    l_chip[pl.ds(chip, 1), :, :] = (l_core[...] + l_pair[...])[None]
    lg_copies = [
        send(l_chip.at[chip], l_chip.at[chip], lg_send.at[j - 1], lg_recv.at[j - 1], peers[j - 1])
        for j in range(1, chips)
    ]

    q_copy.wait_recv()
    qo_ref[...] = t_full[1]
    z_third()
    g_copy.wait_recv()
    tgo_ref[...] = t_full[0]
    for copy in lg_copies:
        copy.wait_recv()
    loss_ref[...] = sum(l_chip[j] for j in range(chips))

    for copy in pending:
        copy.wait_send()


def fused(tokens, cotangent, index, codebook, scale, block, chips, tokens_total, codes_total):
    rows, width = tokens.shape
    code_rows = codebook.shape[0]
    data = RING * RING
    span = code_rows // data
    hs = span // 2
    half = rows // 2
    piece = half // chips
    blocks = code_rows // block
    dma = pltpu.SemaphoreType.DMA
    return pl.pallas_call(
        functools.partial(fused_kernel, scale, code_rows, block, chips, tokens_total, codes_total),
        out_shape=(
            jax.ShapeDtypeStruct((rows, width), BF16),
            jax.ShapeDtypeStruct((rows, width), BF16),
            jax.ShapeDtypeStruct((span, width), BF16),
            jax.ShapeDtypeStruct((1, span), F32),
            jax.ShapeDtypeStruct((1, 128), F32),
        ),
        in_specs=[vmem()] * 3 + [pl.BlockSpec(memory_space=pl.ANY)],
        out_specs=(vmem(),) * 5,
        scratch_shapes=[
            pltpu.VMEM((code_rows, width), BF16),
            pltpu.VMEM((code_rows, rows), F32),
            pltpu.VMEM((code_rows, rows), F32),
            pltpu.VMEM((code_rows, width), F32),
            pltpu.VMEM((code_rows, width), BF16),
            pltpu.VMEM((data, 1, span), F32),
            pltpu.VMEM((blocks, 1, rows), F32),
            pltpu.VMEM((4, rows), F32),
            pltpu.VMEM((width, rows), F32),
            pltpu.VMEM((2, rows, width), BF16),
            pltpu.VMEM((4, rows), F32),
            pltpu.VMEM((4, rows), F32),
            pltpu.VMEM((chips, 4, rows), F32),
            pltpu.VMEM((4, rows), F32),
            pltpu.VMEM((2, half, width), BF16),
            pltpu.VMEM((2, half, width), BF16),
            pltpu.VMEM((2, chips, piece, width), BF16),
            pltpu.VMEM((2, piece, width), BF16),
            pltpu.VMEM((2, rows, width), BF16),
            pltpu.VMEM((RING, 2, hs, width), BF16),
            pltpu.VMEM((RING, 2, hs, width), BF16),
            pltpu.VMEM((RING, 4, hs, width), BF16),
            pltpu.VMEM((RING - 1, 2, hs, width), BF16),
            pltpu.VMEM((2, hs, width), BF16),
            pltpu.VMEM((2, hs, width), BF16),
            pltpu.VMEM((4, hs, width), BF16),
            pltpu.VMEM((data, 1, span), F32),
            pltpu.VMEM((1, 128), F32),
            pltpu.VMEM((data, 1, 128), F32),
            pltpu.VMEM((1, 128), F32),
            pltpu.VMEM((1, 128), F32),
            pltpu.VMEM((chips, 1, 128), F32),
            dma((blocks,)),
            dma, dma,
            dma((chips - 1,)), dma((chips - 1,)),
            dma((2,)), dma((2,)),
            dma((2, chips - 1)), dma((2, chips - 1)),
            dma((2, chips - 1)), dma((2, chips - 1)),
            dma((2,)), dma((2,)),
            dma((RING, 6)), dma((RING, 6)),
            dma((6,)), dma((6,)),
            dma((data - 1,)), dma((data - 1,)),
            dma((data - 1,)), dma((data - 1,)),
            dma, dma,
            dma((chips - 1,)), dma((chips - 1,)),
        ],
        compiler_params=pltpu.CompilerParams(
            collective_id=0, has_side_effects=True, vmem_limit_bytes=VMEM_BYTES
        ),
        name="fused",
    )(tokens, cotangent, index, codebook)


def finish_kernel(*refs):
    count = len(refs) // 2
    for source, target in zip(refs[:count], refs[count:]):
        target[...] = source[...]


def finish(*arrays):
    return pl.pallas_call(
        finish_kernel,
        out_shape=tuple(jax.ShapeDtypeStruct(a.shape, a.dtype) for a in arrays),
        in_specs=[vmem()] * len(arrays),
        out_specs=(vmem(),) * len(arrays),
        name="finish",
    )(*arrays)


def body(block, tokens, codebook, cotangent, index):
    token_rows, features = tokens.shape
    code_rows = codebook.shape[0]
    scale = float(features) ** (-0.5)
    code_devices = lax.axis_size("code")
    data_devices = lax.axis_size("dp")
    results = fused(
        tokens, cotangent, index.reshape(1, token_rows), codebook, scale, block, code_devices // 2,
        token_rows * data_devices, code_rows * code_devices,
    )
    quantized, token_grad, code_sum, code_usage, loss = finish(*results)
    return (quantized, token_grad, code_sum, code_usage.reshape(-1), loss[0, 0])


def solution(mesh, block=512):
    placed = (P("dp", None), P("code", None), P("dp", None), P("dp"))
    return jax.shard_map(
        functools.partial(body, block),
        mesh=mesh,
        in_specs=placed,
        out_specs=(P("dp", None), P("dp", None), P(("code", "dp"), None), P(("code", "dp")), P()),
        check_vma=False,
    )
```

```python
import functools

import jax
import jax.numpy as jnp
from jax import lax
from jax.experimental import pallas as pl
from jax.experimental.pallas import tpu as pltpu
from jax.sharding import PartitionSpec as P

MESH = pl.DeviceIdType.MESH
F32 = jnp.float32
BF16 = jnp.bfloat16
RING = 4
VMEM_BYTES = 60 * 1024 * 1024


def dot(a, b, dims):
    return lax.dot_general(a, b, (dims, ((), ())), preferred_element_type=F32)


def vmem():
    return pl.BlockSpec(memory_space=pltpu.VMEM)


def fused_kernel(
    scale, code_rows, block, chips, tokens_total, codes_total,
    tok_ref, cot_ref, idx_ref, cb_hbm,
    qo_ref, tgo_ref, cgo_ref, uso_ref, loss_ref,
    cb_ref, w_buf, s_buf, ch_buf, cg_ref, us_ref, tops, run, acc, qt_ref,
    pair_buf, mine_buf, chip_buf, stats,
    t_in, t_half, t_piece, t_sum, t_full,
    x_hop, x_out, x_got, z_part, z_hop, z_out, z_got,
    u_buf, l_own, l_all, l_dp, l_core, l_pair, l_chip,
    cb_sem, s_send, s_recv, st_send, st_recv,
    t_send, t_recv, p_send, p_recv, g_send, g_recv, f_send, f_recv,
    x_send, x_recv, z_send, z_recv,
    u_sems, ld_send, ld_recv, lc_send, lc_recv, lg_send, lg_recv,
):
    dp = lax.axis_index("dp")
    code = lax.axis_index("code")
    core, chip = code % 2, code // 2
    xi, zi = dp // RING, dp % RING
    data = RING * RING
    blocks = code_rows // block
    rows = tok_ref.shape[0]
    half = rows // 2
    piece = half // chips
    span = code_rows // data
    hs = span // 2
    first_code = code * code_rows

    def load(i):
        part = pl.ds(pl.multiple_of(i * block, block), block)
        return pltpu.make_async_copy(cb_hbm.at[part], cb_ref.at[part], cb_sem.at[i])

    for i in range(blocks):
        load(i).start()

    partner = (dp, chip * 2 + 1 - core)
    peers = [(dp, ((chip + j) % chips) * 2 + core) for j in range(1, chips)]
    mates = [((dp + j) % data, code) for j in range(1, data)]
    xn = {d: (((xi + d) % RING) * RING + zi, code) for d in (1, 3)}
    zn = {d: (xi * RING + (zi + d) % RING, code) for d in (1, 3)}

    barrier = pltpu.get_barrier_semaphore()
    for peer in [partner] + peers + mates:
        pl.semaphore_signal(barrier, inc=1, device_id=peer, device_id_type=MESH)

    pending = []

    def send(src, dst, ssem, rsem, peer):
        copy = pltpu.make_async_remote_copy(
            src_ref=src, dst_ref=dst, send_sem=ssem, recv_sem=rsem, device_id=peer, device_id_type=MESH
        )
        copy.start()
        pending.append(copy)
        return copy

    run[0:1, :] = jnp.full((1, rows), -jnp.inf, F32)
    run[1:4, :] = jnp.zeros((3, rows), F32)

    def totals(i, carry):
        load(i).wait()
        part = pl.ds(pl.multiple_of(i * block, block), block)
        codes = cb_ref[part, :]
        logits = dot(codes, tok_ref[...], ((1,), (1,)))
        sensed = dot(codes, cot_ref[...], ((1,), (1,)))
        old = run[0:1, :]
        top = jnp.maximum(old, jnp.max(logits, axis=0, keepdims=True))
        weights = jnp.exp((logits - top) * scale)
        factor = jnp.exp((old - top) * scale)
        w_buf[part, :] = weights
        s_buf[part, :] = sensed
        tops[i] = top
        run[0:1, :] = top
        run[1:2, :] = run[1:2, :] * factor + jnp.sum(weights, axis=0, keepdims=True)
        run[2:3, :] = run[2:3, :] * factor + jnp.sum(weights * sensed, axis=0, keepdims=True)
        run[3:4, :] = run[3:4, :] * factor + jnp.sum(weights * logits, axis=0, keepdims=True)
        return carry

    lax.fori_loop(0, blocks, totals, 0)

    pl.semaphore_wait(barrier, chips + data - 1)
    swap = send(run, pair_buf, s_send, s_recv, partner)

    acc[...] = jnp.zeros_like(acc)

    def picks(i, carry):
        part = pl.ds(pl.multiple_of(i * block, block), block)
        ids = lax.broadcasted_iota(jnp.int32, (block, rows), 0)
        hot = jnp.where(ids == idx_ref[...] - (first_code + i * block), 1.0, 0.0).astype(BF16)
        acc[...] += dot(cb_ref[part, :], hot, ((0,), (0,)))
        ch_buf[part, :] = dot(hot, cot_ref[...], ((1,), (0,)))
        return carry

    lax.fori_loop(0, blocks // 4, picks, 0)

    swap.wait_recv()
    one, two = run[...], pair_buf[...]
    top = jnp.maximum(one[0:1], two[0:1])
    mine_buf[0:1, :] = top
    mine_buf[1:4, :] = one[1:4] * jnp.exp((one[0:1] - top) * scale) + two[1:4] * jnp.exp((two[0:1] - top) * scale)
    st_copies = [
        send(mine_buf, chip_buf.at[chip], st_send.at[j - 1], st_recv.at[j - 1], peers[j - 1])
        for j in range(1, chips)
    ]
    chip_buf[pl.ds(chip, 1), :, :] = mine_buf[...][None]

    lax.fori_loop(blocks // 4, blocks, picks, 0)

    theirs = pl.ds(pl.multiple_of((1 - core) * half, half), half)
    ours = pl.ds(pl.multiple_of(core * half, half), half)

    def rows_of(j):
        return pl.ds(pl.multiple_of(((chip + j) % chips) * piece, piece), piece)

    def t_core(a):
        return send(qt_ref.at[a, theirs], t_in.at[a], t_send.at[a], t_recv.at[a], partner)

    def t_scatter(a, copy):
        copy.wait_recv()
        t_half[a] = (t_in[a].astype(F32) + qt_ref[a, ours, :].astype(F32)).astype(BF16)
        return [
            send(t_half.at[a, rows_of(j)], t_piece.at[a, j], p_send.at[a, j - 1], p_recv.at[a, j - 1], peers[j - 1])
            for j in range(1, chips)
        ]

    def t_gather(a, copies):
        for copy in copies:
            copy.wait_recv()
        total = t_half[a, rows_of(0), :].astype(F32)
        for j in range(1, chips):
            total = total + t_piece[a, j].astype(F32)
        t_sum[a] = total.astype(BF16)
        spot = pl.ds(pl.multiple_of(core * half + chip * piece, piece), piece)
        sent = [
            send(t_sum.at[a], t_full.at[a, spot], g_send.at[a, j - 1], g_recv.at[a, j - 1], peers[j - 1])
            for j in range(1, chips)
        ]
        t_full[a, spot, :] = t_sum[a]
        return sent

    def t_share(a, copies):
        for copy in copies:
            copy.wait_recv()
        return send(t_full.at[a, ours], t_full.at[a, ours], f_send.at[a], f_recv.at[a], partner)

    qt_ref[1] = acc[...].T.astype(BF16)
    q_copy = t_core(1)
    acc[...] = jnp.zeros_like(acc)

    for copy in st_copies:
        copy.wait_recv()
    peaks = [chip_buf[j, 0:1, :] for j in range(chips)]
    peak = functools.reduce(jnp.maximum, peaks)
    total = sum(chip_buf[j, 1:4, :] * jnp.exp((peaks[j] - peak) * scale) for j in range(chips))
    weight = total[0:1]
    stats[0:1, :] = peak
    stats[1:2, :] = 1.0 / weight
    stats[2:3, :] = total[1:2] / weight
    stats[3:4, :] = jnp.log(weight) + (peak - total[2:3] / weight) * scale

    order = [(zi + d) % RING for d in (2, 1, 3, 0)]
    lanes = min(128, rows)

    def units(k, low, high):
        def unit(i, carry):
            owner = ((xi + 6 - i) % RING) * RING + order[k]
            start = owner * span
            part = pl.ds(pl.multiple_of(start, span), span)
            level = jnp.exp((tops[start // block] - stats[0:1, :]) * scale) * stats[1:2, :]
            probs = w_buf[part, :] * level
            grad = (probs * (s_buf[part, :] - stats[2:3, :])).astype(BF16)
            acc[...] += dot(cb_ref[part, :], grad, ((0,), (0,)))
            cg_ref[part, :] = (dot(grad, tok_ref[...], ((1,), (0,))) * scale + ch_buf[part, :]).astype(BF16)
            folded = sum(probs[:, c : c + lanes] for c in range(0, rows, lanes))
            us_ref[owner] = jnp.sum(folded.T, axis=0, keepdims=True)
            return carry

        lax.fori_loop(low, high, unit, 0, unroll=True)

    x_copies = {}
    z_copies = {}

    def part(xd, k, side):
        start = (((xi + xd) % RING) * RING + order[k]) * span + side * hs
        return pl.ds(pl.multiple_of(start, hs), hs)

    def x_first(k):
        x_copies[k, 0] = send(cg_ref.at[part(2, k, 0)], x_hop.at[k, 0], x_send.at[k, 0], x_recv.at[k, 0], xn[1])
        x_copies[k, 1] = send(cg_ref.at[part(2, k, 1)], x_hop.at[k, 1], x_send.at[k, 1], x_recv.at[k, 1], xn[3])

    def x_direct(k):
        x_copies[k, 2] = send(cg_ref.at[part(1, k, 1)], x_got.at[k, 1], x_send.at[k, 2], x_recv.at[k, 2], xn[1])
        x_copies[k, 3] = send(cg_ref.at[part(3, k, 0)], x_got.at[k, 0], x_send.at[k, 3], x_recv.at[k, 3], xn[3])

    def x_second(k):
        x_copies[k, 0].wait_recv()
        x_out[k, 0] = (x_hop[k, 0].astype(F32) + cg_ref[part(1, k, 0), :].astype(F32)).astype(BF16)
        x_copies[k, 4] = send(x_out.at[k, 0], x_got.at[k, 3], x_send.at[k, 4], x_recv.at[k, 4], xn[1])
        x_copies[k, 1].wait_recv()
        x_out[k, 1] = (x_hop[k, 1].astype(F32) + cg_ref[part(3, k, 1), :].astype(F32)).astype(BF16)
        x_copies[k, 5] = send(x_out.at[k, 1], x_got.at[k, 2], x_send.at[k, 5], x_recv.at[k, 5], xn[3])

    def x_third(k):
        for i in (2, 3, 4, 5):
            x_copies[k, i].wait_recv()
        low = cg_ref[part(0, k, 0), :].astype(F32) + x_got[k, 0].astype(F32) + x_got[k, 3].astype(F32)
        high = cg_ref[part(0, k, 1), :].astype(F32) + x_got[k, 1].astype(F32) + x_got[k, 2].astype(F32)
        return low, high

    def z_store(k):
        low, high = x_third(k)
        z_part[k, 0] = low.astype(BF16)
        z_part[k, 1] = high.astype(BF16)

    def z_first():
        z_store(0)
        z_copies[0] = send(z_part.at[0, 0], z_hop.at[0], z_send.at[0], z_recv.at[0], zn[1])
        z_copies[1] = send(z_part.at[0, 1], z_hop.at[1], z_send.at[1], z_recv.at[1], zn[3])

    def z_second_up():
        z_store(1)
        z_copies[2] = send(z_part.at[1, 1], z_got.at[1], z_send.at[2], z_recv.at[2], zn[1])
        z_copies[0].wait_recv()
        z_out[0] = (z_hop[0].astype(F32) + z_part[1, 0].astype(F32)).astype(BF16)
        z_copies[4] = send(z_out.at[0], z_got.at[3], z_send.at[4], z_recv.at[4], zn[1])

    def z_second_down():
        z_store(2)
        z_copies[3] = send(z_part.at[2, 0], z_got.at[0], z_send.at[3], z_recv.at[3], zn[3])
        z_copies[1].wait_recv()
        z_out[1] = (z_hop[1].astype(F32) + z_part[2, 1].astype(F32)).astype(BF16)
        z_copies[5] = send(z_out.at[1], z_got.at[2], z_send.at[5], z_recv.at[5], zn[3])

    def z_third():
        low, high = x_third(3)
        for i in (2, 3, 4, 5):
            z_copies[i].wait_recv()
        cgo_ref[0:hs, :] = (low + z_got[0].astype(F32) + z_got[3].astype(F32)).astype(BF16)
        cgo_ref[hs:, :] = (high + z_got[1].astype(F32) + z_got[2].astype(F32)).astype(BF16)

    u_copies = []

    def u_send(k):
        for xd in range(RING if k < RING - 1 else 1, 2 * RING if k < RING - 1 else RING):
            owner = ((xi + xd) % RING) * RING + order[k]
            slot = k * RING + xd % RING
            u_copies.append(
                send(us_ref.at[owner], u_buf.at[dp], u_sems.at[0, slot], u_sems.at[1, slot], (owner, code))
            )

    units(0, 0, 1)
    x_first(0)
    q_copies = t_scatter(1, q_copy)
    units(0, 1, 4)
    u_send(0)
    x_direct(0)
    units(1, 0, 4)
    u_send(1)
    x_first(1)
    x_second(0)
    x_direct(1)
    units(2, 0, 4)
    u_send(2)
    x_first(2)
    q_copies = t_gather(1, q_copies)
    units(3, 0, 4)
    u_send(3)
    qt_ref[0] = (acc[...] * scale).T.astype(BF16)
    g_copy = t_core(0)
    u_buf[pl.ds(dp, 1), :, :] = us_ref[pl.ds(dp, 1), :, :]
    x_second(1)
    x_direct(2)
    x_first(3)
    g_copies = t_scatter(0, g_copy)
    q_copy = t_share(1, q_copies)
    z_first()
    x_second(2)
    x_direct(3)

    for copy in u_copies:
        copy.wait_recv()
    usage = sum(u_buf[j] for j in range(data))
    uso_ref[...] = usage * (codes_total / tokens_total)
    shares = usage / tokens_total
    terms = jnp.where(shares > 0, shares * jnp.log(jnp.where(shares > 0, shares, 1.0)), 0.0)
    local = jnp.sum(stats[3:4, :]) / (tokens_total * chips * 2) + jnp.sum(terms)
    l_core[...] = jnp.full(l_core.shape, local, F32)
    lc_copy = send(l_core, l_pair, lc_send, lc_recv, partner)
    z_second_up()
    lc_copy.wait_recv()
    l_own[...] = l_core[...] + l_pair[...]
    l_chip[pl.ds(chip, 1), :, :] = l_own[...][None]
    lg_copies = [
        send(l_own, l_chip.at[chip], lg_send.at[j - 1], lg_recv.at[j - 1], peers[j - 1]) for j in range(1, chips)
    ]
    x_second(3)
    g_copies = t_gather(0, g_copies)
    z_second_down()
    for copy in lg_copies:
        copy.wait_recv()
    l_all[...] = sum(l_chip[j] for j in range(chips))
    l_dp[pl.ds(dp, 1), :, :] = l_all[...][None]
    ld_copies = [
        send(l_all, l_dp.at[dp], ld_send.at[j - 1], ld_recv.at[j - 1], mates[j - 1]) for j in range(1, data)
    ]
    q_copy.wait_recv()
    qo_ref[...] = t_full[1]
    z_third()
    g_copy = t_share(0, g_copies)
    for copy in ld_copies:
        copy.wait_recv()
    loss_ref[...] = sum(l_dp[j] for j in range(data))
    g_copy.wait_recv()
    tgo_ref[...] = t_full[0]

    for copy in pending:
        copy.wait_send()


def fused(tokens, cotangent, index, codebook, scale, block, chips, tokens_total, codes_total):
    rows, width = tokens.shape
    code_rows = codebook.shape[0]
    data = RING * RING
    span = code_rows // data
    hs = span // 2
    half = rows // 2
    piece = half // chips
    blocks = code_rows // block
    dma = pltpu.SemaphoreType.DMA
    return pl.pallas_call(
        functools.partial(fused_kernel, scale, code_rows, block, chips, tokens_total, codes_total),
        out_shape=(
            jax.ShapeDtypeStruct((rows, width), BF16),
            jax.ShapeDtypeStruct((rows, width), BF16),
            jax.ShapeDtypeStruct((span, width), BF16),
            jax.ShapeDtypeStruct((1, span), F32),
            jax.ShapeDtypeStruct((1, 128), F32),
        ),
        in_specs=[vmem()] * 3 + [pl.BlockSpec(memory_space=pl.ANY)],
        out_specs=(vmem(),) * 5,
        scratch_shapes=[
            pltpu.VMEM((code_rows, width), BF16),
            pltpu.VMEM((code_rows, rows), F32),
            pltpu.VMEM((code_rows, rows), F32),
            pltpu.VMEM((code_rows, width), F32),
            pltpu.VMEM((code_rows, width), BF16),
            pltpu.VMEM((data, 1, span), F32),
            pltpu.VMEM((blocks, 1, rows), F32),
            pltpu.VMEM((4, rows), F32),
            pltpu.VMEM((width, rows), F32),
            pltpu.VMEM((2, rows, width), BF16),
            pltpu.VMEM((4, rows), F32),
            pltpu.VMEM((4, rows), F32),
            pltpu.VMEM((chips, 4, rows), F32),
            pltpu.VMEM((4, rows), F32),
            pltpu.VMEM((2, half, width), BF16),
            pltpu.VMEM((2, half, width), BF16),
            pltpu.VMEM((2, chips, piece, width), BF16),
            pltpu.VMEM((2, piece, width), BF16),
            pltpu.VMEM((2, rows, width), BF16),
            pltpu.VMEM((RING, 2, hs, width), BF16),
            pltpu.VMEM((RING, 2, hs, width), BF16),
            pltpu.VMEM((RING, 4, hs, width), BF16),
            pltpu.VMEM((RING - 1, 2, hs, width), BF16),
            pltpu.VMEM((2, hs, width), BF16),
            pltpu.VMEM((2, hs, width), BF16),
            pltpu.VMEM((4, hs, width), BF16),
            pltpu.VMEM((data, 1, span), F32),
            pltpu.VMEM((1, 128), F32),
            pltpu.VMEM((1, 128), F32),
            pltpu.VMEM((data, 1, 128), F32),
            pltpu.VMEM((1, 128), F32),
            pltpu.VMEM((1, 128), F32),
            pltpu.VMEM((chips, 1, 128), F32),
            dma((blocks,)),
            dma, dma,
            dma((chips - 1,)), dma((chips - 1,)),
            dma((2,)), dma((2,)),
            dma((2, chips - 1)), dma((2, chips - 1)),
            dma((2, chips - 1)), dma((2, chips - 1)),
            dma((2,)), dma((2,)),
            dma((RING, 6)), dma((RING, 6)),
            dma((6,)), dma((6,)),
            dma((2, data)),
            dma((data - 1,)), dma((data - 1,)),
            dma, dma,
            dma((chips - 1,)), dma((chips - 1,)),
        ],
        compiler_params=pltpu.CompilerParams(
            collective_id=0, has_side_effects=True, vmem_limit_bytes=VMEM_BYTES
        ),
        name="fused",
    )(tokens, cotangent, index, codebook)


def finish_kernel(*refs):
    count = len(refs) // 2
    for source, target in zip(refs[:count], refs[count:]):
        target[...] = source[...]


def finish(*arrays):
    return pl.pallas_call(
        finish_kernel,
        out_shape=tuple(jax.ShapeDtypeStruct(a.shape, a.dtype) for a in arrays),
        in_specs=[vmem()] * len(arrays),
        out_specs=(vmem(),) * len(arrays),
        name="finish",
    )(*arrays)


def body(block, tokens, codebook, cotangent, index):
    token_rows, features = tokens.shape
    code_rows = codebook.shape[0]
    scale = float(features) ** (-0.5)
    code_devices = lax.axis_size("code")
    data_devices = lax.axis_size("dp")
    results = fused(
        tokens, cotangent, index.reshape(1, token_rows), codebook, scale, block, code_devices // 2,
        token_rows * data_devices, code_rows * code_devices,
    )
    quantized, token_grad, code_sum, code_usage, loss = finish(*results)
    return (quantized, token_grad, code_sum, code_usage.reshape(-1), loss[0, 0])


def solution(mesh, block=512):
    placed = (P("dp", None), P("code", None), P("dp", None), P("dp"))
    return jax.shard_map(
        functools.partial(body, block),
        mesh=mesh,
        in_specs=placed,
        out_specs=(P("dp", None), P("dp", None), P(("code", "dp"), None), P(("code", "dp")), P()),
        check_vma=False,
    )
```

```python
import functools

import jax
import jax.numpy as jnp
from jax import lax
from jax.experimental import pallas as pl
from jax.experimental.pallas import tpu as pltpu
from jax.sharding import PartitionSpec as P

MESH = pl.DeviceIdType.MESH
F32 = jnp.float32
BF16 = jnp.bfloat16
RING = 4
VMEM_BYTES = 60 * 1024 * 1024


def dot(a, b, dims):
    return lax.dot_general(a, b, (dims, ((), ())), preferred_element_type=F32)


def vmem():
    return pl.BlockSpec(memory_space=pltpu.VMEM)


def fused_kernel(
    scale, code_rows, block, chips, tokens_total, codes_total,
    tok_ref, cot_ref, idx_ref, cb_hbm,
    qo_ref, tgo_ref, cgo_ref, uso_ref, loss_ref,
    cb_ref, w_buf, s_buf, ch_buf, cg_ref, us_ref, tops, run, acc, qt_ref,
    pair_buf, mine_buf, chip_buf, stats,
    t_in, t_half, t_piece, t_sum, t_full,
    x_hop, x_out, x_got, z_part, z_hop, z_out, z_got,
    u_buf, l_own, l_all, l_dp, l_core, l_pair, l_chip,
    cb_sem, s_send, s_recv, st_send, st_recv,
    t_send, t_recv, p_send, p_recv, g_send, g_recv, f_send, f_recv,
    x_send, x_recv, z_send, z_recv,
    u_sems, ld_send, ld_recv, lc_send, lc_recv, lg_send, lg_recv,
):
    dp = lax.axis_index("dp")
    code = lax.axis_index("code")
    core, chip = code % 2, code // 2
    xi, zi = dp // RING, dp % RING
    data = RING * RING
    blocks = code_rows // block
    rows = tok_ref.shape[0]
    half = rows // 2
    piece = half // chips
    span = code_rows // data
    hs = span // 2
    first_code = code * code_rows

    def load(i):
        part = pl.ds(pl.multiple_of(i * block, block), block)
        return pltpu.make_async_copy(cb_hbm.at[part], cb_ref.at[part], cb_sem.at[i])

    for i in range(blocks):
        load(i).start()

    partner = (dp, chip * 2 + 1 - core)
    peers = [(dp, ((chip + j) % chips) * 2 + core) for j in range(1, chips)]
    mates = [((dp + j) % data, code) for j in range(1, data)]
    xn = {d: (((xi + d) % RING) * RING + zi, code) for d in (1, 3)}
    zn = {d: (xi * RING + (zi + d) % RING, code) for d in (1, 3)}

    barrier = pltpu.get_barrier_semaphore()
    for peer in [partner] + peers + mates:
        pl.semaphore_signal(barrier, inc=1, device_id=peer, device_id_type=MESH)

    pending = []

    def send(src, dst, ssem, rsem, peer):
        copy = pltpu.make_async_remote_copy(
            src_ref=src, dst_ref=dst, send_sem=ssem, recv_sem=rsem, device_id=peer, device_id_type=MESH
        )
        copy.start()
        pending.append(copy)
        return copy

    run[0:1, :] = jnp.full((1, rows), -jnp.inf, F32)
    run[1:4, :] = jnp.zeros((3, rows), F32)

    def totals(i, carry):
        load(i).wait()
        part = pl.ds(pl.multiple_of(i * block, block), block)
        codes = cb_ref[part, :]
        logits = dot(codes, tok_ref[...], ((1,), (1,)))
        sensed = dot(codes, cot_ref[...], ((1,), (1,)))
        old = run[0:1, :]
        top = jnp.maximum(old, jnp.max(logits, axis=0, keepdims=True))
        weights = jnp.exp((logits - top) * scale)
        factor = jnp.exp((old - top) * scale)
        w_buf[part, :] = weights
        s_buf[part, :] = sensed
        tops[i] = top
        run[0:1, :] = top
        run[1:2, :] = run[1:2, :] * factor + jnp.sum(weights, axis=0, keepdims=True)
        run[2:3, :] = run[2:3, :] * factor + jnp.sum(weights * sensed, axis=0, keepdims=True)
        run[3:4, :] = run[3:4, :] * factor + jnp.sum(weights * logits, axis=0, keepdims=True)
        return carry

    lax.fori_loop(0, blocks, totals, 0)

    pl.semaphore_wait(barrier, chips + data - 1)
    swap = send(run, pair_buf, s_send, s_recv, partner)

    acc[...] = jnp.zeros_like(acc)

    def picks(i, carry):
        part = pl.ds(pl.multiple_of(i * block, block), block)
        ids = lax.broadcasted_iota(jnp.int32, (block, rows), 0)
        hot = jnp.where(ids == idx_ref[...] - (first_code + i * block), 1.0, 0.0).astype(BF16)
        acc[...] += dot(cb_ref[part, :], hot, ((0,), (0,)))
        ch_buf[part, :] = dot(hot, cot_ref[...], ((1,), (0,)))
        return carry

    lax.fori_loop(0, blocks // 4, picks, 0)

    swap.wait_recv()
    one, two = run[...], pair_buf[...]
    top = jnp.maximum(one[0:1], two[0:1])
    mine_buf[0:1, :] = top
    mine_buf[1:4, :] = one[1:4] * jnp.exp((one[0:1] - top) * scale) + two[1:4] * jnp.exp((two[0:1] - top) * scale)
    st_copies = [
        send(mine_buf, chip_buf.at[chip], st_send.at[j - 1], st_recv.at[j - 1], peers[j - 1])
        for j in range(1, chips)
    ]
    chip_buf[pl.ds(chip, 1), :, :] = mine_buf[...][None]

    lax.fori_loop(blocks // 4, blocks, picks, 0)

    theirs = pl.ds(pl.multiple_of((1 - core) * half, half), half)
    ours = pl.ds(pl.multiple_of(core * half, half), half)

    def rows_of(j):
        return pl.ds(pl.multiple_of(((chip + j) % chips) * piece, piece), piece)

    def t_core(a):
        return send(qt_ref.at[a, theirs], t_in.at[a], t_send.at[a], t_recv.at[a], partner)

    def t_scatter(a, copy):
        copy.wait_recv()
        t_half[a] = (t_in[a].astype(F32) + qt_ref[a, ours, :].astype(F32)).astype(BF16)
        return [
            send(t_half.at[a, rows_of(j)], t_piece.at[a, j], p_send.at[a, j - 1], p_recv.at[a, j - 1], peers[j - 1])
            for j in range(1, chips)
        ]

    def t_gather(a, copies):
        for copy in copies:
            copy.wait_recv()
        total = t_half[a, rows_of(0), :].astype(F32)
        for j in range(1, chips):
            total = total + t_piece[a, j].astype(F32)
        t_sum[a] = total.astype(BF16)
        spot = pl.ds(pl.multiple_of(core * half + chip * piece, piece), piece)
        sent = [
            send(t_sum.at[a], t_full.at[a, spot], g_send.at[a, j - 1], g_recv.at[a, j - 1], peers[j - 1])
            for j in range(1, chips)
        ]
        t_full[a, spot, :] = t_sum[a]
        return sent

    def t_share(a, copies):
        for copy in copies:
            copy.wait_recv()
        return send(t_full.at[a, ours], t_full.at[a, ours], f_send.at[a], f_recv.at[a], partner)

    qt_ref[1] = acc[...].T.astype(BF16)
    q_copy = t_core(1)
    acc[...] = jnp.zeros_like(acc)

    for copy in st_copies:
        copy.wait_recv()
    peaks = [chip_buf[j, 0:1, :] for j in range(chips)]
    peak = functools.reduce(jnp.maximum, peaks)
    total = sum(chip_buf[j, 1:4, :] * jnp.exp((peaks[j] - peak) * scale) for j in range(chips))
    weight = total[0:1]
    stats[0:1, :] = peak
    stats[1:2, :] = 1.0 / weight
    stats[2:3, :] = total[1:2] / weight
    stats[3:4, :] = jnp.log(weight) + (peak - total[2:3] / weight) * scale

    order = [(zi + d) % RING for d in (2, 1, 3, 0)]
    lanes = min(128, rows)

    def units(k, low, high):
        def unit(i, carry):
            owner = ((xi + 6 - i) % RING) * RING + order[k]
            start = owner * span
            part = pl.ds(pl.multiple_of(start, span), span)
            level = jnp.exp((tops[start // block] - stats[0:1, :]) * scale) * stats[1:2, :]
            probs = w_buf[part, :] * level
            grad = (probs * (s_buf[part, :] - stats[2:3, :])).astype(BF16)
            acc[...] += dot(cb_ref[part, :], grad, ((0,), (0,)))
            cg_ref[part, :] = (dot(grad, tok_ref[...], ((1,), (0,))) * scale + ch_buf[part, :]).astype(BF16)
            return carry

        lax.fori_loop(low, high, unit, 0, unroll=True)

    def usage_of(owner, carry):
        start = owner * span
        level = jnp.exp((tops[start // block] - stats[0:1, :]) * scale) * stats[1:2, :]
        probs = w_buf[pl.ds(pl.multiple_of(start, span), span), :] * level
        folded = sum(probs[:, c : c + lanes] for c in range(0, rows, lanes))
        us_ref[owner] = jnp.sum(folded.T, axis=0, keepdims=True)
        return carry

    x_copies = {}
    z_copies = {}

    def part(xd, k, side):
        start = (((xi + xd) % RING) * RING + order[k]) * span + side * hs
        return pl.ds(pl.multiple_of(start, hs), hs)

    def x_first(k):
        x_copies[k, 0] = send(cg_ref.at[part(2, k, 0)], x_hop.at[k, 0], x_send.at[k, 0], x_recv.at[k, 0], xn[1])
        x_copies[k, 1] = send(cg_ref.at[part(2, k, 1)], x_hop.at[k, 1], x_send.at[k, 1], x_recv.at[k, 1], xn[3])

    def x_direct(k):
        x_copies[k, 2] = send(cg_ref.at[part(1, k, 1)], x_got.at[k, 1], x_send.at[k, 2], x_recv.at[k, 2], xn[1])
        x_copies[k, 3] = send(cg_ref.at[part(3, k, 0)], x_got.at[k, 0], x_send.at[k, 3], x_recv.at[k, 3], xn[3])

    def x_second(k):
        x_copies[k, 0].wait_recv()
        x_out[k, 0] = (x_hop[k, 0].astype(F32) + cg_ref[part(1, k, 0), :].astype(F32)).astype(BF16)
        x_copies[k, 4] = send(x_out.at[k, 0], x_got.at[k, 3], x_send.at[k, 4], x_recv.at[k, 4], xn[1])
        x_copies[k, 1].wait_recv()
        x_out[k, 1] = (x_hop[k, 1].astype(F32) + cg_ref[part(3, k, 1), :].astype(F32)).astype(BF16)
        x_copies[k, 5] = send(x_out.at[k, 1], x_got.at[k, 2], x_send.at[k, 5], x_recv.at[k, 5], xn[3])

    def x_third(k):
        for i in (2, 3, 4, 5):
            x_copies[k, i].wait_recv()
        low = cg_ref[part(0, k, 0), :].astype(F32) + x_got[k, 0].astype(F32) + x_got[k, 3].astype(F32)
        high = cg_ref[part(0, k, 1), :].astype(F32) + x_got[k, 1].astype(F32) + x_got[k, 2].astype(F32)
        return low, high

    def z_store(k):
        low, high = x_third(k)
        z_part[k, 0] = low.astype(BF16)
        z_part[k, 1] = high.astype(BF16)

    def z_first():
        z_store(0)
        z_copies[0] = send(z_part.at[0, 0], z_hop.at[0], z_send.at[0], z_recv.at[0], zn[1])
        z_copies[1] = send(z_part.at[0, 1], z_hop.at[1], z_send.at[1], z_recv.at[1], zn[3])

    def z_second_up():
        z_store(1)
        z_copies[2] = send(z_part.at[1, 1], z_got.at[1], z_send.at[2], z_recv.at[2], zn[1])
        z_copies[0].wait_recv()
        z_out[0] = (z_hop[0].astype(F32) + z_part[1, 0].astype(F32)).astype(BF16)
        z_copies[4] = send(z_out.at[0], z_got.at[3], z_send.at[4], z_recv.at[4], zn[1])

    def z_second_down():
        z_store(2)
        z_copies[3] = send(z_part.at[2, 0], z_got.at[0], z_send.at[3], z_recv.at[3], zn[3])
        z_copies[1].wait_recv()
        z_out[1] = (z_hop[1].astype(F32) + z_part[2, 1].astype(F32)).astype(BF16)
        z_copies[5] = send(z_out.at[1], z_got.at[2], z_send.at[5], z_recv.at[5], zn[3])

    def z_third():
        low, high = x_third(3)
        for i in (2, 3, 4, 5):
            z_copies[i].wait_recv()
        cgo_ref[0:hs, :] = (low + z_got[0].astype(F32) + z_got[3].astype(F32)).astype(BF16)
        cgo_ref[hs:, :] = (high + z_got[1].astype(F32) + z_got[2].astype(F32)).astype(BF16)

    units(0, 0, 1)
    x_first(0)

    lax.fori_loop(0, data, usage_of, 0, unroll=4)
    u_copies = [
        send(us_ref.at[(dp + j) % data], u_buf.at[dp], u_sems.at[0, j], u_sems.at[1, j], mates[j - 1])
        for j in range(1, data)
    ]
    u_buf[pl.ds(dp, 1), :, :] = us_ref[pl.ds(dp, 1), :, :]

    q_copies = t_scatter(1, q_copy)
    units(0, 1, 4)
    x_direct(0)
    units(1, 0, 4)
    x_first(1)
    x_second(0)
    x_direct(1)
    units(2, 0, 4)
    x_first(2)
    q_copies = t_gather(1, q_copies)
    units(3, 0, 4)
    qt_ref[0] = (acc[...] * scale).T.astype(BF16)
    g_copy = t_core(0)

    for copy in u_copies:
        copy.wait_recv()
    usage = sum(u_buf[j] for j in range(data))
    uso_ref[...] = usage * (codes_total / tokens_total)
    shares = usage / tokens_total
    terms = jnp.where(shares > 0, shares * jnp.log(jnp.where(shares > 0, shares, 1.0)), 0.0)
    local = jnp.sum(stats[3:4, :]) / (tokens_total * chips * 2) + jnp.sum(terms)
    l_core[...] = jnp.full(l_core.shape, local, F32)
    lc_copy = send(l_core, l_pair, lc_send, lc_recv, partner)

    x_second(1)
    x_direct(2)
    x_first(3)
    g_copies = t_scatter(0, g_copy)
    lc_copy.wait_recv()
    l_own[...] = l_core[...] + l_pair[...]
    l_chip[pl.ds(chip, 1), :, :] = l_own[...][None]
    lg_copies = [
        send(l_own, l_chip.at[chip], lg_send.at[j - 1], lg_recv.at[j - 1], peers[j - 1]) for j in range(1, chips)
    ]
    z_first()
    x_second(2)
    x_direct(3)
    q_copy = t_share(1, q_copies)
    for copy in lg_copies:
        copy.wait_recv()
    l_all[...] = sum(l_chip[j] for j in range(chips))
    l_dp[pl.ds(dp, 1), :, :] = l_all[...][None]
    ld_copies = [
        send(l_all, l_dp.at[dp], ld_send.at[j - 1], ld_recv.at[j - 1], mates[j - 1]) for j in range(1, data)
    ]
    z_second_up()
    x_second(3)
    g_copies = t_gather(0, g_copies)
    z_second_down()
    q_copy.wait_recv()
    qo_ref[...] = t_full[1]
    g_copy = t_share(0, g_copies)
    z_third()
    for copy in ld_copies:
        copy.wait_recv()
    loss_ref[...] = sum(l_dp[j] for j in range(data))
    g_copy.wait_recv()
    tgo_ref[...] = t_full[0]

    for copy in pending:
        copy.wait_send()


def fused(tokens, cotangent, index, codebook, scale, block, chips, tokens_total, codes_total):
    rows, width = tokens.shape
    code_rows = codebook.shape[0]
    data = RING * RING
    span = code_rows // data
    hs = span // 2
    half = rows // 2
    piece = half // chips
    blocks = code_rows // block
    dma = pltpu.SemaphoreType.DMA
    return pl.pallas_call(
        functools.partial(fused_kernel, scale, code_rows, block, chips, tokens_total, codes_total),
        out_shape=(
            jax.ShapeDtypeStruct((rows, width), BF16),
            jax.ShapeDtypeStruct((rows, width), BF16),
            jax.ShapeDtypeStruct((span, width), BF16),
            jax.ShapeDtypeStruct((1, span), F32),
            jax.ShapeDtypeStruct((1, 128), F32),
        ),
        in_specs=[vmem()] * 3 + [pl.BlockSpec(memory_space=pl.ANY)],
        out_specs=(vmem(),) * 5,
        scratch_shapes=[
            pltpu.VMEM((code_rows, width), BF16),
            pltpu.VMEM((code_rows, rows), F32),
            pltpu.VMEM((code_rows, rows), F32),
            pltpu.VMEM((code_rows, width), F32),
            pltpu.VMEM((code_rows, width), BF16),
            pltpu.VMEM((data, 1, span), F32),
            pltpu.VMEM((blocks, 1, rows), F32),
            pltpu.VMEM((4, rows), F32),
            pltpu.VMEM((width, rows), F32),
            pltpu.VMEM((2, rows, width), BF16),
            pltpu.VMEM((4, rows), F32),
            pltpu.VMEM((4, rows), F32),
            pltpu.VMEM((chips, 4, rows), F32),
            pltpu.VMEM((4, rows), F32),
            pltpu.VMEM((2, half, width), BF16),
            pltpu.VMEM((2, half, width), BF16),
            pltpu.VMEM((2, chips, piece, width), BF16),
            pltpu.VMEM((2, piece, width), BF16),
            pltpu.VMEM((2, rows, width), BF16),
            pltpu.VMEM((RING, 2, hs, width), BF16),
            pltpu.VMEM((RING, 2, hs, width), BF16),
            pltpu.VMEM((RING, 4, hs, width), BF16),
            pltpu.VMEM((RING - 1, 2, hs, width), BF16),
            pltpu.VMEM((2, hs, width), BF16),
            pltpu.VMEM((2, hs, width), BF16),
            pltpu.VMEM((4, hs, width), BF16),
            pltpu.VMEM((data, 1, span), F32),
            pltpu.VMEM((1, 128), F32),
            pltpu.VMEM((1, 128), F32),
            pltpu.VMEM((data, 1, 128), F32),
            pltpu.VMEM((1, 128), F32),
            pltpu.VMEM((1, 128), F32),
            pltpu.VMEM((chips, 1, 128), F32),
            dma((blocks,)),
            dma, dma,
            dma((chips - 1,)), dma((chips - 1,)),
            dma((2,)), dma((2,)),
            dma((2, chips - 1)), dma((2, chips - 1)),
            dma((2, chips - 1)), dma((2, chips - 1)),
            dma((2,)), dma((2,)),
            dma((RING, 6)), dma((RING, 6)),
            dma((6,)), dma((6,)),
            dma((2, data)),
            dma((data - 1,)), dma((data - 1,)),
            dma, dma,
            dma((chips - 1,)), dma((chips - 1,)),
        ],
        compiler_params=pltpu.CompilerParams(
            collective_id=0, has_side_effects=True, vmem_limit_bytes=VMEM_BYTES
        ),
        name="fused",
    )(tokens, cotangent, index, codebook)


def finish_kernel(*refs):
    count = len(refs) // 2
    for source, target in zip(refs[:count], refs[count:]):
        target[...] = source[...]


def finish(*arrays):
    return pl.pallas_call(
        finish_kernel,
        out_shape=tuple(jax.ShapeDtypeStruct(a.shape, a.dtype) for a in arrays),
        in_specs=[vmem()] * len(arrays),
        out_specs=(vmem(),) * len(arrays),
        name="finish",
    )(*arrays)


def body(block, tokens, codebook, cotangent, index):
    token_rows, features = tokens.shape
    code_rows = codebook.shape[0]
    scale = float(features) ** (-0.5)
    code_devices = lax.axis_size("code")
    data_devices = lax.axis_size("dp")
    results = fused(
        tokens, cotangent, index.reshape(1, token_rows), codebook, scale, block, code_devices // 2,
        token_rows * data_devices, code_rows * code_devices,
    )
    quantized, token_grad, code_sum, code_usage, loss = finish(*results)
    return (quantized, token_grad, code_sum, code_usage.reshape(-1), loss[0, 0])


def solution(mesh, block=512):
    placed = (P("dp", None), P("code", None), P("dp", None), P("dp"))
    return jax.shard_map(
        functools.partial(body, block),
        mesh=mesh,
        in_specs=placed,
        out_specs=(P("dp", None), P("dp", None), P(("code", "dp"), None), P(("code", "dp")), P()),
        check_vma=False,
    )
```

```python
import functools

import jax
import jax.numpy as jnp
from jax import lax
from jax.experimental import pallas as pl
from jax.experimental.pallas import tpu as pltpu
from jax.sharding import PartitionSpec as P

MESH = pl.DeviceIdType.MESH
F32 = jnp.float32
BF16 = jnp.bfloat16
RING = 4
VMEM_BYTES = 60 * 1024 * 1024


def dot(a, b, dims):
    return lax.dot_general(a, b, (dims, ((), ())), preferred_element_type=F32)


def vmem():
    return pl.BlockSpec(memory_space=pltpu.VMEM)


def fused_kernel(
    scale, code_rows, block, chips, tokens_total, codes_total,
    tok_ref, cot_ref, idx_ref, cb_hbm,
    qo_ref, tgo_ref, cgo_ref, uso_ref, loss_ref,
    cb_ref, l_buf, w_buf, s_buf, ch_buf, cg_ref, us_ref, tops, run, acc, qt_ref,
    pair_buf, mine_buf, chip_buf, stats,
    t_in, t_half, t_piece, t_sum, t_full,
    x_hop, x_out, x_got, z_part, z_hop, z_out, z_got,
    u_buf, l_own, l_all, l_dp, l_core, l_pair, l_chip,
    cb_sem, s_send, s_recv, st_send, st_recv,
    t_send, t_recv, p_send, p_recv, g_send, g_recv, f_send, f_recv,
    x_send, x_recv, z_send, z_recv,
    u_sems, ld_send, ld_recv, lc_send, lc_recv, lg_send, lg_recv,
):
    dp = lax.axis_index("dp")
    code = lax.axis_index("code")
    core, chip = code % 2, code // 2
    xi, zi = dp // RING, dp % RING
    data = RING * RING
    blocks = code_rows // block
    rows = tok_ref.shape[0]
    half = rows // 2
    piece = half // chips
    span = code_rows // data
    hs = span // 2
    first_code = code * code_rows

    def load(i):
        part = pl.ds(pl.multiple_of(i * block, block), block)
        return pltpu.make_async_copy(cb_hbm.at[part], cb_ref.at[part], cb_sem.at[i])

    for i in range(blocks):
        load(i).start()

    partner = (dp, chip * 2 + 1 - core)
    peers = [(dp, ((chip + j) % chips) * 2 + core) for j in range(1, chips)]
    mates = [((dp + j) % data, code) for j in range(1, data)]
    xn = {d: (((xi + d) % RING) * RING + zi, code) for d in (1, 3)}
    zn = {d: (xi * RING + (zi + d) % RING, code) for d in (1, 3)}

    barrier = pltpu.get_barrier_semaphore()
    for peer in [partner] + peers + mates:
        pl.semaphore_signal(barrier, inc=1, device_id=peer, device_id_type=MESH)

    pending = []

    def send(src, dst, ssem, rsem, peer):
        copy = pltpu.make_async_remote_copy(
            src_ref=src, dst_ref=dst, send_sem=ssem, recv_sem=rsem, device_id=peer, device_id_type=MESH
        )
        copy.start()
        pending.append(copy)
        return copy

    run[0:1, :] = jnp.full((1, rows), -jnp.inf, F32)
    run[1:4, :] = jnp.zeros((3, rows), F32)

    strip = min(64, block)

    def products(i):
        load(i).wait()
        part = slice(i * block, (i + 1) * block)
        codes = cb_ref[part, :]
        l_buf[i % 2] = dot(codes, tok_ref[...], ((1,), (1,)))
        s_buf[part, :] = dot(codes, cot_ref[...], ((1,), (1,)))

    def totals(i):
        old = run[0:1, :]
        top = jnp.maximum(old, jnp.max(l_buf[i % 2], axis=0, keepdims=True))
        factor = jnp.exp((old - top) * scale)
        sums = [jnp.zeros((8, rows), F32)] * 3
        for low in range(0, block, strip):
            part = slice(i * block + low, i * block + low + strip)
            logits = l_buf[i % 2, low : low + strip, :]
            weights = jnp.exp2((logits - top) * (scale * 1.4426950408889634))
            w_buf[part, :] = weights
            for n, term in enumerate((weights, weights * s_buf[part, :], weights * logits)):
                sums[n] = sums[n] + jnp.sum(term.reshape(strip // 8, 8, rows), axis=0)
        tops[i] = top
        run[0:1, :] = top
        for n in range(3):
            run[n + 1 : n + 2, :] = run[n + 1 : n + 2, :] * factor + jnp.sum(sums[n], axis=0, keepdims=True)

    products(0)
    for i in range(blocks):
        if i + 1 < blocks:
            products(i + 1)
        totals(i)

    pl.semaphore_wait(barrier, chips + data - 1)
    swap = send(run, pair_buf, s_send, s_recv, partner)

    acc[...] = jnp.zeros_like(acc)

    def picks(i, carry):
        part = pl.ds(pl.multiple_of(i * block, block), block)
        ids = lax.broadcasted_iota(jnp.int32, (block, rows), 0)
        hot = jnp.where(ids == idx_ref[...] - (first_code + i * block), 1.0, 0.0).astype(BF16)
        acc[...] += dot(cb_ref[part, :], hot, ((0,), (0,)))
        ch_buf[part, :] = dot(hot, cot_ref[...], ((1,), (0,)))
        return carry

    lax.fori_loop(0, blocks // 4, picks, 0)

    swap.wait_recv()
    one, two = run[...], pair_buf[...]
    top = jnp.maximum(one[0:1], two[0:1])
    mine_buf[0:1, :] = top
    mine_buf[1:4, :] = one[1:4] * jnp.exp((one[0:1] - top) * scale) + two[1:4] * jnp.exp((two[0:1] - top) * scale)
    st_copies = [
        send(mine_buf, chip_buf.at[chip], st_send.at[j - 1], st_recv.at[j - 1], peers[j - 1])
        for j in range(1, chips)
    ]
    chip_buf[pl.ds(chip, 1), :, :] = mine_buf[...][None]

    lax.fori_loop(blocks // 4, blocks, picks, 0)

    theirs = pl.ds(pl.multiple_of((1 - core) * half, half), half)
    ours = pl.ds(pl.multiple_of(core * half, half), half)

    def rows_of(j):
        return pl.ds(pl.multiple_of(((chip + j) % chips) * piece, piece), piece)

    def t_core(a):
        return send(qt_ref.at[a, theirs], t_in.at[a], t_send.at[a], t_recv.at[a], partner)

    def t_scatter(a, copy):
        copy.wait_recv()
        t_half[a] = (t_in[a].astype(F32) + qt_ref[a, ours, :].astype(F32)).astype(BF16)
        return [
            send(t_half.at[a, rows_of(j)], t_piece.at[a, j], p_send.at[a, j - 1], p_recv.at[a, j - 1], peers[j - 1])
            for j in range(1, chips)
        ]

    def t_gather(a, copies):
        for copy in copies:
            copy.wait_recv()
        total = t_half[a, rows_of(0), :].astype(F32)
        for j in range(1, chips):
            total = total + t_piece[a, j].astype(F32)
        t_sum[a] = total.astype(BF16)
        spot = pl.ds(pl.multiple_of(core * half + chip * piece, piece), piece)
        sent = [
            send(t_sum.at[a], t_full.at[a, spot], g_send.at[a, j - 1], g_recv.at[a, j - 1], peers[j - 1])
            for j in range(1, chips)
        ]
        t_full[a, spot, :] = t_sum[a]
        return sent

    def t_share(a, copies):
        for copy in copies:
            copy.wait_recv()
        return send(t_full.at[a, ours], t_full.at[a, ours], f_send.at[a], f_recv.at[a], partner)

    qt_ref[1] = acc[...].T.astype(BF16)
    q_copy = t_core(1)
    acc[...] = jnp.zeros_like(acc)

    for copy in st_copies:
        copy.wait_recv()
    peaks = [chip_buf[j, 0:1, :] for j in range(chips)]
    peak = functools.reduce(jnp.maximum, peaks)
    total = sum(chip_buf[j, 1:4, :] * jnp.exp((peaks[j] - peak) * scale) for j in range(chips))
    weight = total[0:1]
    stats[0:1, :] = peak
    stats[1:2, :] = 1.0 / weight
    stats[2:3, :] = total[1:2] / weight
    stats[3:4, :] = jnp.log(weight) + (peak - total[2:3] / weight) * scale

    order = [(zi + d) % RING for d in (2, 1, 3, 0)]
    lanes = min(128, rows)

    def units(k, low, high):
        def unit(i, carry):
            owner = ((xi + 6 - i) % RING) * RING + order[k]
            start = owner * span
            part = pl.ds(pl.multiple_of(start, span), span)
            level = jnp.exp((tops[start // block] - stats[0:1, :]) * scale) * stats[1:2, :]
            probs = w_buf[part, :] * level
            grad = (probs * (s_buf[part, :] - stats[2:3, :])).astype(BF16)
            acc[...] += dot(cb_ref[part, :], grad, ((0,), (0,)))
            cg_ref[part, :] = (dot(grad, tok_ref[...], ((1,), (0,))) * scale + ch_buf[part, :]).astype(BF16)
            return carry

        lax.fori_loop(low, high, unit, 0, unroll=True)

    def usage_of(owner, carry):
        start = owner * span
        level = jnp.exp((tops[start // block] - stats[0:1, :]) * scale) * stats[1:2, :]
        probs = w_buf[pl.ds(pl.multiple_of(start, span), span), :] * level
        folded = sum(probs[:, c : c + lanes] for c in range(0, rows, lanes))
        us_ref[owner] = jnp.sum(folded.T, axis=0, keepdims=True)
        return carry

    x_copies = {}
    z_copies = {}

    def part(xd, k, side):
        start = (((xi + xd) % RING) * RING + order[k]) * span + side * hs
        return pl.ds(pl.multiple_of(start, hs), hs)

    def x_first(k):
        x_copies[k, 0] = send(cg_ref.at[part(2, k, 0)], x_hop.at[k, 0], x_send.at[k, 0], x_recv.at[k, 0], xn[1])
        x_copies[k, 1] = send(cg_ref.at[part(2, k, 1)], x_hop.at[k, 1], x_send.at[k, 1], x_recv.at[k, 1], xn[3])

    def x_direct(k):
        x_copies[k, 2] = send(cg_ref.at[part(1, k, 1)], x_got.at[k, 1], x_send.at[k, 2], x_recv.at[k, 2], xn[1])
        x_copies[k, 3] = send(cg_ref.at[part(3, k, 0)], x_got.at[k, 0], x_send.at[k, 3], x_recv.at[k, 3], xn[3])

    def x_second(k):
        x_copies[k, 0].wait_recv()
        x_out[k, 0] = (x_hop[k, 0].astype(F32) + cg_ref[part(1, k, 0), :].astype(F32)).astype(BF16)
        x_copies[k, 4] = send(x_out.at[k, 0], x_got.at[k, 3], x_send.at[k, 4], x_recv.at[k, 4], xn[1])
        x_copies[k, 1].wait_recv()
        x_out[k, 1] = (x_hop[k, 1].astype(F32) + cg_ref[part(3, k, 1), :].astype(F32)).astype(BF16)
        x_copies[k, 5] = send(x_out.at[k, 1], x_got.at[k, 2], x_send.at[k, 5], x_recv.at[k, 5], xn[3])

    def x_third(k):
        for i in (2, 3, 4, 5):
            x_copies[k, i].wait_recv()
        low = cg_ref[part(0, k, 0), :].astype(F32) + x_got[k, 0].astype(F32) + x_got[k, 3].astype(F32)
        high = cg_ref[part(0, k, 1), :].astype(F32) + x_got[k, 1].astype(F32) + x_got[k, 2].astype(F32)
        return low, high

    def z_store(k):
        low, high = x_third(k)
        z_part[k, 0] = low.astype(BF16)
        z_part[k, 1] = high.astype(BF16)

    def z_first():
        z_store(0)
        z_copies[0] = send(z_part.at[0, 0], z_hop.at[0], z_send.at[0], z_recv.at[0], zn[1])
        z_copies[1] = send(z_part.at[0, 1], z_hop.at[1], z_send.at[1], z_recv.at[1], zn[3])

    def z_second_up():
        z_store(1)
        z_copies[2] = send(z_part.at[1, 1], z_got.at[1], z_send.at[2], z_recv.at[2], zn[1])
        z_copies[0].wait_recv()
        z_out[0] = (z_hop[0].astype(F32) + z_part[1, 0].astype(F32)).astype(BF16)
        z_copies[4] = send(z_out.at[0], z_got.at[3], z_send.at[4], z_recv.at[4], zn[1])

    def z_second_down():
        z_store(2)
        z_copies[3] = send(z_part.at[2, 0], z_got.at[0], z_send.at[3], z_recv.at[3], zn[3])
        z_copies[1].wait_recv()
        z_out[1] = (z_hop[1].astype(F32) + z_part[2, 1].astype(F32)).astype(BF16)
        z_copies[5] = send(z_out.at[1], z_got.at[2], z_send.at[5], z_recv.at[5], zn[3])

    def z_third():
        low, high = x_third(3)
        for i in (2, 3, 4, 5):
            z_copies[i].wait_recv()
        cgo_ref[0:hs, :] = (low + z_got[0].astype(F32) + z_got[3].astype(F32)).astype(BF16)
        cgo_ref[hs:, :] = (high + z_got[1].astype(F32) + z_got[2].astype(F32)).astype(BF16)

    units(0, 0, 1)
    x_first(0)

    lax.fori_loop(0, data, usage_of, 0, unroll=4)
    u_copies = [
        send(us_ref.at[(dp + j) % data], u_buf.at[dp], u_sems.at[0, j], u_sems.at[1, j], mates[j - 1])
        for j in range(1, data)
    ]
    u_buf[pl.ds(dp, 1), :, :] = us_ref[pl.ds(dp, 1), :, :]

    q_copies = t_scatter(1, q_copy)
    units(0, 1, 4)
    x_direct(0)
    units(1, 0, 4)
    x_first(1)
    x_second(0)
    x_direct(1)
    units(2, 0, 4)
    x_first(2)
    q_copies = t_gather(1, q_copies)
    units(3, 0, 4)
    qt_ref[0] = (acc[...] * scale).T.astype(BF16)
    g_copy = t_core(0)

    for copy in u_copies:
        copy.wait_recv()
    usage = sum(u_buf[j] for j in range(data))
    uso_ref[...] = usage * (codes_total / tokens_total)
    shares = usage / tokens_total
    terms = jnp.where(shares > 0, shares * jnp.log(jnp.where(shares > 0, shares, 1.0)), 0.0)
    local = jnp.sum(stats[3:4, :]) / (tokens_total * chips * 2) + jnp.sum(terms)
    l_core[...] = jnp.full(l_core.shape, local, F32)
    lc_copy = send(l_core, l_pair, lc_send, lc_recv, partner)

    x_second(1)
    x_direct(2)
    x_first(3)
    g_copies = t_scatter(0, g_copy)
    lc_copy.wait_recv()
    l_own[...] = l_core[...] + l_pair[...]
    l_chip[pl.ds(chip, 1), :, :] = l_own[...][None]
    lg_copies = [
        send(l_own, l_chip.at[chip], lg_send.at[j - 1], lg_recv.at[j - 1], peers[j - 1]) for j in range(1, chips)
    ]
    z_first()
    x_second(2)
    x_direct(3)
    q_copy = t_share(1, q_copies)
    for copy in lg_copies:
        copy.wait_recv()
    l_all[...] = sum(l_chip[j] for j in range(chips))
    l_dp[pl.ds(dp, 1), :, :] = l_all[...][None]
    ld_copies = [
        send(l_all, l_dp.at[dp], ld_send.at[j - 1], ld_recv.at[j - 1], mates[j - 1]) for j in range(1, data)
    ]
    z_second_up()
    x_second(3)
    g_copies = t_gather(0, g_copies)
    z_second_down()
    q_copy.wait_recv()
    qo_ref[...] = t_full[1]
    g_copy = t_share(0, g_copies)
    z_third()
    for copy in ld_copies:
        copy.wait_recv()
    loss_ref[...] = sum(l_dp[j] for j in range(data))
    g_copy.wait_recv()
    tgo_ref[...] = t_full[0]

    for copy in pending:
        copy.wait_send()


def fused(tokens, cotangent, index, codebook, scale, block, chips, tokens_total, codes_total):
    rows, width = tokens.shape
    code_rows = codebook.shape[0]
    data = RING * RING
    span = code_rows // data
    hs = span // 2
    half = rows // 2
    piece = half // chips
    blocks = code_rows // block
    dma = pltpu.SemaphoreType.DMA
    return pl.pallas_call(
        functools.partial(fused_kernel, scale, code_rows, block, chips, tokens_total, codes_total),
        out_shape=(
            jax.ShapeDtypeStruct((rows, width), BF16),
            jax.ShapeDtypeStruct((rows, width), BF16),
            jax.ShapeDtypeStruct((span, width), BF16),
            jax.ShapeDtypeStruct((1, span), F32),
            jax.ShapeDtypeStruct((1, 128), F32),
        ),
        in_specs=[vmem()] * 3 + [pl.BlockSpec(memory_space=pl.ANY)],
        out_specs=(vmem(),) * 5,
        scratch_shapes=[
            pltpu.VMEM((code_rows, width), BF16),
            pltpu.VMEM((2, block, rows), F32),
            pltpu.VMEM((code_rows, rows), F32),
            pltpu.VMEM((code_rows, rows), F32),
            pltpu.VMEM((code_rows, width), F32),
            pltpu.VMEM((code_rows, width), BF16),
            pltpu.VMEM((data, 1, span), F32),
            pltpu.VMEM((blocks, 1, rows), F32),
            pltpu.VMEM((4, rows), F32),
            pltpu.VMEM((width, rows), F32),
            pltpu.VMEM((2, rows, width), BF16),
            pltpu.VMEM((4, rows), F32),
            pltpu.VMEM((4, rows), F32),
            pltpu.VMEM((chips, 4, rows), F32),
            pltpu.VMEM((4, rows), F32),
            pltpu.VMEM((2, half, width), BF16),
            pltpu.VMEM((2, half, width), BF16),
            pltpu.VMEM((2, chips, piece, width), BF16),
            pltpu.VMEM((2, piece, width), BF16),
            pltpu.VMEM((2, rows, width), BF16),
            pltpu.VMEM((RING, 2, hs, width), BF16),
            pltpu.VMEM((RING, 2, hs, width), BF16),
            pltpu.VMEM((RING, 4, hs, width), BF16),
            pltpu.VMEM((RING - 1, 2, hs, width), BF16),
            pltpu.VMEM((2, hs, width), BF16),
            pltpu.VMEM((2, hs, width), BF16),
            pltpu.VMEM((4, hs, width), BF16),
            pltpu.VMEM((data, 1, span), F32),
            pltpu.VMEM((1, 128), F32),
            pltpu.VMEM((1, 128), F32),
            pltpu.VMEM((data, 1, 128), F32),
            pltpu.VMEM((1, 128), F32),
            pltpu.VMEM((1, 128), F32),
            pltpu.VMEM((chips, 1, 128), F32),
            dma((blocks,)),
            dma, dma,
            dma((chips - 1,)), dma((chips - 1,)),
            dma((2,)), dma((2,)),
            dma((2, chips - 1)), dma((2, chips - 1)),
            dma((2, chips - 1)), dma((2, chips - 1)),
            dma((2,)), dma((2,)),
            dma((RING, 6)), dma((RING, 6)),
            dma((6,)), dma((6,)),
            dma((2, data)),
            dma((data - 1,)), dma((data - 1,)),
            dma, dma,
            dma((chips - 1,)), dma((chips - 1,)),
        ],
        compiler_params=pltpu.CompilerParams(
            collective_id=0, has_side_effects=True, vmem_limit_bytes=VMEM_BYTES
        ),
        name="fused",
    )(tokens, cotangent, index, codebook)


def finish_kernel(*refs):
    count = len(refs) // 2
    for source, target in zip(refs[:count], refs[count:]):
        target[...] = source[...]


def finish(*arrays):
    return pl.pallas_call(
        finish_kernel,
        out_shape=tuple(jax.ShapeDtypeStruct(a.shape, a.dtype) for a in arrays),
        in_specs=[vmem()] * len(arrays),
        out_specs=(vmem(),) * len(arrays),
        name="finish",
    )(*arrays)


def body(block, tokens, codebook, cotangent, index):
    token_rows, features = tokens.shape
    code_rows = codebook.shape[0]
    scale = float(features) ** (-0.5)
    code_devices = lax.axis_size("code")
    data_devices = lax.axis_size("dp")
    results = fused(
        tokens, cotangent, index.reshape(1, token_rows), codebook, scale, block, code_devices // 2,
        token_rows * data_devices, code_rows * code_devices,
    )
    quantized, token_grad, code_sum, code_usage, loss = finish(*results)
    return (quantized, token_grad, code_sum, code_usage.reshape(-1), loss[0, 0])


def solution(mesh, block=512):
    placed = (P("dp", None), P("code", None), P("dp", None), P("dp"))
    return jax.shard_map(
        functools.partial(body, block),
        mesh=mesh,
        in_specs=placed,
        out_specs=(P("dp", None), P("dp", None), P(("code", "dp"), None), P(("code", "dp")), P()),
        check_vma=False,
    )
```
